768 devices in a mesh: grp: 16 (over y, core), own: 48 (over x, z).
Axes of the slice: x: 4, y: 8, z: 12, core: 2. Of those that a mesh axis runs over, the one named last changes fastest.
Arguments:
- fields: bfloat16 [192, 256, 128], P(None, 'grp'), may hold values from -6 to 6
- labels: int32 [192], replicated, may hold values 0 or 1
- pair_first: int32 [16, 48, 16], P('grp', 'own'), may hold values from 0 to 255, as said below
- pair_second: int32 [16, 48, 16], P(None, 'own'), may hold values from 0 to 255, as said below
- pair_count: int32 [16, 48], P('grp', 'own'), may hold values from 4 to 16, as said below
- pair_mats: float32 [16, 48, 16, 128, 128], P('grp', 'own'), may hold values from -6 to 6
Outputs:
- logits: float32 [192], replicated
- field_grad: float32 [192, 256, 128], P('own', 'grp')
- new_mats: float32 [16, 48, 16, 128, 128], P('grp', 'own')
The draws below stay inside these ranges and needn't reach their ends.
Inputs may be any that keep to these rules, and one draw needn't show every extreme that they name: pair_first[g, o, s] lies in the block of fields g * 16 to (g + 1) * 16 - 1. `pair_second`: on every device (g, o), each block of 16 fields holds the second field of exactly 1 of the 16 slots; the second field is never the first. `pair_count`: slots at and beyond the count hold no pair; one device has all 16 slots live.
All inputs are finite; a program needn't handle non-finite values.
Results may differ from the reference program's by a relative error of at most 0.0003.
Values may be sent and summed in bfloat16 or wider, within the bound.
No kernel may reach another device: no remote copies, remote signals or barrier semaphores. Data moves between devices by JAX's collectives and lax.ppermute only.
A program may use at most 32 MiB of HBM per device.

```python
import math
import jax
import jax.numpy as jnp
from jax import lax

K = 128
F = 256
B = 192
SLOTS = 16
STEPS = 2
N_GRP = 16
N_OWN = 48


def pair_tables(key):
    key_order, key_first, key_second, key_count, key_full = jax.random.split(jax.random.fold_in(key, 7), 5)
    capacity = SLOTS // N_GRP
    per_block = F // N_GRP
    shape_all = (N_GRP, N_OWN, SLOTS)
    base_blocks = jnp.arange(SLOTS, dtype=jnp.int32) // capacity
    scores = jax.random.randint(key_order, shape_all, 0, 1 << 20) * SLOTS + jnp.arange(SLOTS, dtype=jnp.int32)
    ordering = jnp.argsort(scores, axis=-1)
    block_ids = base_blocks[ordering]
    first_off = jax.random.randint(key_first, shape_all, 0, per_block)
    second_off = (first_off + 1 + jax.random.randint(key_second, shape_all, 0, per_block - 1)) % per_block
    group_ids = jnp.arange(N_GRP, dtype=jnp.int32)[:, None, None]
    first_ids = group_ids * per_block + first_off
    second_ids = block_ids * per_block + second_off
    counts = jax.random.randint(key_count, (N_GRP, N_OWN), SLOTS // 4, SLOTS * 5 // 8 + 1)
    full_device = jax.random.randint(key_full, (), 0, N_GRP * N_OWN)
    device_ids = jnp.arange(N_GRP * N_OWN, dtype=jnp.int32).reshape(N_GRP, N_OWN)
    counts = jnp.where(device_ids == full_device, SLOTS, counts)
    return (first_ids.astype(jnp.int32), second_ids.astype(jnp.int32), counts.astype(jnp.int32))


def draw_pair_first(key, part):
    return pair_tables(key)[0]


def draw_pair_second(key, part):
    return pair_tables(key)[1]


def draw_pair_count(key, part):
    return pair_tables(key)[2]


def place_ends(result, stream_key, least, top_value):
    longest = result.shape.index(max(result.shape))
    spots = []
    for shift in (0, 1):
        where = [jax.random.randint(jax.random.fold_in(stream_key, axis), (), 0, length) for axis, length in enumerate(result.shape)]
        where[longest] = (where[longest] + shift) % result.shape[longest]
        spots.append(tuple(where))
    return result.at[spots[0]].set(least).at[spots[1]].set(top_value)


def levels(own_key, dims, pieces, least, high):
    def one(position, blocks):
        steps = jax.random.uniform(jax.random.fold_in(jax.random.fold_in(own_key, 6), position), (blocks,), jnp.float32, least / len(pieces), high / len(pieces))
        return jnp.repeat(jnp.exp(steps), dims[position] // blocks).reshape((-1,) + (1,) * (len(dims) - position - 1))

    factor_of = one(*pieces[0])
    for cut in pieces[1:]:
        factor_of = factor_of * one(*cut)
    return factor_of


def gaussian(rng, shape, width, bound, pieces=(), kind=jnp.bfloat16):
    array = width * jax.random.normal(rng, shape, jnp.float32)
    if pieces:
        array = array * levels(rng, shape, pieces, -0.22, 0.18)
    return jnp.clip(array, -bound, bound).astype(kind)


def setup_inputs(seed: int = 0) -> dict:
    keys = jax.random.split(jax.random.key(seed), 7)
    fields = gaussian(keys[0], (B, F, K), 1.0, 6.0, ((1, 16),))
    labels = place_ends((jax.random.randint(keys[1], (B,), 0, 2) < 1).astype(jnp.int32), jax.random.fold_in(keys[1], 1), 0, 1)
    pair_first = draw_pair_first(jax.random.fold_in(keys[6], 71), 0)
    pair_second = draw_pair_second(jax.random.fold_in(keys[6], 71), 0)
    pair_count = draw_pair_count(jax.random.fold_in(keys[6], 71), 0)
    pair_mats = gaussian(keys[5], (N_GRP, N_OWN, SLOTS, K, K), 1.0, 6.0, ((0, 16), (1, 48)), jnp.float32)
    return dict(fields=fields, labels=labels, pair_first=pair_first, pair_second=pair_second, pair_count=pair_count, pair_mats=pair_mats)


logit_gain = 1.5
step_size = 1000.0
highest = lax.Precision.HIGHEST

def device_view(field_data, first_ids, second_ids, matrices):
    first_vec = jnp.take(field_data, first_ids, axis=1)
    second_vec = jnp.take(field_data, second_ids, axis=1)
    mixed = jnp.einsum('bsk,skl->bsl', first_vec, matrices, precision=highest)
    return (first_vec, second_vec, mixed)

def reference(fields, labels, pair_first, pair_second, pair_count, pair_mats):
    groups, owners, slot_count = pair_first.shape
    devices = groups * owners
    samples, _, feature = fields.shape
    field_data = fields.astype(jnp.float32)
    targets = labels.astype(jnp.float32)
    firsts = pair_first.reshape(devices, slot_count)
    seconds = pair_second.reshape(devices, slot_count)
    live_mask = (jnp.arange(slot_count, dtype=jnp.int32)[None, :] < pair_count.reshape(devices, 1)).astype(jnp.float32)
    matrices = pair_mats.reshape(devices, slot_count, feature, feature)
    logit_scale = logit_gain / math.sqrt(devices * slot_count)
    root_width = math.sqrt(feature)
    logits = jnp.zeros((samples,), jnp.float32)
    dense_grad = jnp.zeros(fields.shape, jnp.float32)
    for step_index in range(STEPS):

        def partial_of(accum, device_item):
            first_ids, second_ids, alive, mats_here = device_item
            first_vec, second_vec, mixed = device_view(field_data, first_ids, second_ids, mats_here)
            partial_value = lax.optimization_barrier(jnp.sum(lax.optimization_barrier(jnp.sum(mixed * second_vec, axis=2)) / feature * alive[None, :], axis=1))
            return (accum + partial_value, None)
        total_sum, _ = lax.scan(partial_of, jnp.zeros((samples,), jnp.float32), (firsts, seconds, live_mask, matrices))
        logits = logit_scale * total_sum
        errors = jax.nn.sigmoid(logits) - targets
        last_step = step_index == STEPS - 1

        def update_of(accum, device_item):
            first_ids, second_ids, alive, mats_here = device_item
            first_vec, second_vec, mixed = device_view(field_data, first_ids, second_ids, mats_here)
            if last_step:
                grad_first = errors[:, None, None] * jnp.einsum('skl,bsl->bsk', mats_here, second_vec, precision=highest) / root_width * alive[None, :, None]
                grad_second = errors[:, None, None] * mixed / root_width * alive[None, :, None]
                accum = accum.at[:, first_ids].add(grad_first).at[:, second_ids].add(grad_second)
            gradient = jnp.einsum('bsk,bsl->skl', first_vec * errors[:, None, None], second_vec, precision=highest)
            updated = mats_here - step_size * logit_scale / (samples * feature) * alive[:, None, None] * gradient
            return (accum, updated)
        dense_grad, matrices = lax.scan(update_of, jnp.zeros(fields.shape, jnp.float32), (firsts, seconds, live_mask, matrices))
    return (logits, dense_grad, matrices.reshape(pair_mats.shape))
```

```python
import functools
import math

import jax
import jax.numpy as jnp
from jax import lax
from jax.experimental import pallas as pl
from jax.experimental.pallas import tpu as pltpu
from jax.sharding import Mesh
from jax.sharding import PartitionSpec as P

GRP = ("y", "core")
OWN = ("x", "z")
logit_gain = 1.5
step_size = 1000.0
f32 = jnp.float32
bf16 = jnp.bfloat16

SLOT, FIRST, LIVE, SERVED, ME = range(5)


def split(x):
    hi = x.astype(bf16)
    return hi, (x - hi.astype(f32)).astype(bf16)


def dot(a, b, dims):
    return lax.dot_general(a, b, (dims, ((), ())), preferred_element_type=f32)


def dot_rhs(a, pair, dims):
    return dot(a, pair[0], dims) + dot(a, pair[1], dims)


def dot_lhs(pair, b, dims):
    return dot(pair[0], b, dims) + dot(pair[1], b, dims)


AB, ABT, ATB = ((1,), (0,)), ((1,), (1,)), ((0,), (0,))


def row_sums(acc):
    ones = jnp.ones((8, 128), f32)
    exact = functools.partial(
        lax.dot_general,
        dimension_numbers=(ABT, ((), ())),
        precision=lax.Precision.HIGHEST,
        preferred_element_type=f32,
    )
    low = exact(ones, acc[:128])
    rest = acc[128:]
    high = exact(ones, jnp.concatenate([rest, jnp.zeros((256 - acc.shape[0], 128), f32)], axis=0))
    rows = lax.broadcasted_iota(jnp.int32, (8, 128), 0)
    return jnp.where(rows < 4, low, high)


def spread(chunk, samples):
    low = jnp.transpose(jnp.broadcast_to(chunk[0:1], (128, 128)))
    high = jnp.transpose(jnp.broadcast_to(chunk[4:5], (128, 128)))
    return jnp.concatenate([low, high[: samples - 128]], axis=0)


def gather_kernel(tab, ft, out):
    @pl.loop(0, out.shape[0])
    def _(j):
        out[j] = ft[tab[SERVED, j]]


def partial_kernel(tab, ft, second, mats, out, acc):
    acc[...] = jnp.zeros_like(acc)

    def step(j, carry):
        live = tab[LIVE, j].astype(f32)
        mixed = dot_rhs(ft[tab[FIRST, j]], split(mats[tab[SLOT, j]] * live), AB)
        acc[...] += mixed * second[j].astype(f32)
        return carry

    lax.fori_loop(0, second.shape[0], step, 0, unroll=4)
    chunk = row_sums(acc[...] * (1.0 / 128.0))
    for i in range(out.shape[0]):
        out[i] = chunk


def sum_kernel(parts, out):
    total = parts[0]
    for i in range(1, parts.shape[0]):
        total = total + parts[i]
    for i in range(out.shape[0]):
        out[i] = total


def total_of(parts, lo):
    total = parts[0, lo : lo + 8]
    for i in range(1, parts.shape[0]):
        total = total + parts[i, lo : lo + 8]
    return total


def terms_kernel(
    scale, rate, tab, ft, second, mats, sums, labels, moved, out, dense, acc, errs
):
    samples = second.shape[1]
    n_x, rows = dense.shape[0], samples // dense.shape[0]
    errors = jax.nn.sigmoid(scale * total_of(sums, 0)) - labels[...]
    errs[...] = spread(errors, samples)
    acc[...] = jnp.zeros_like(acc)
    dense[...] = jnp.zeros_like(dense)

    def step(j, carry):
        live = tab[LIVE, j].astype(f32)
        slot, first = tab[SLOT, j], tab[FIRST, j]
        va, vb = ft[first], second[j]
        gradient = dot_lhs(split(va.astype(f32) * errs[...]), vb, ATB)
        updated = mats[slot] - (rate * live) * gradient
        moved[j] = updated
        pair = split(updated * live)
        mixed = dot_rhs(va, pair, AB)
        acc[...] += mixed * vb.astype(f32)
        out[j, 0:samples] = mixed
        toward = dot_rhs(vb, pair, ABT)
        at = pl.ds(pl.multiple_of(first * rows, 8), rows)
        for i in range(n_x):
            dense[i, at] += toward[i * rows : (i + 1) * rows]
        return carry

    lax.fori_loop(0, second.shape[0], step, 0, unroll=2)
    chunk = row_sums(acc[...] * (1.0 / 128.0))
    for i in range(out.shape[0]):
        out[i, samples : samples + 8] = chunk


def dense_kernel(tab, got, dense_in, dense):
    dense[...] = dense_in[...]
    samples = got.shape[1] - 8
    n_x, rows = dense.shape[0], samples // dense.shape[0]
    last = dense.shape[1] - 8

    @pl.loop(0, got.shape[0])
    def _(j):
        at = pl.ds(pl.multiple_of(tab[SERVED, j] * rows, 8), rows)
        for i in range(n_x):
            dense[i, at] += got[j, i * rows : (i + 1) * rows]

    chunk = total_of(got, samples)
    for i in range(n_x):
        dense[i, last : last + 8] = chunk


def across_kernel(got, out):
    n_z, few = out.shape[0], (out.shape[1] - 8) // 16
    rows = n_z * few
    for f in range(16):
        total = got[0, f * rows : (f + 1) * rows]
        for i in range(1, got.shape[0]):
            total = total + got[i, f * rows : (f + 1) * rows]
        for k in range(n_z):
            out[k, f * few : (f + 1) * few] = total[k * few : (k + 1) * few]
    chunk = total_of(got, 16 * rows)
    for k in range(n_z):
        out[k, 16 * few :] = chunk


def last_kernel(
    scale, rate, tab, ft, second, moved, got, labels, logits, grads, mats, errs, sums
):
    samples = second.shape[1]
    few = grads.shape[0]
    value = scale * total_of(got, 16 * few)
    logits[...] = value
    errs[...] = spread(jax.nn.sigmoid(value) - labels[...], samples)
    total = got[0, : 16 * few]
    for i in range(1, got.shape[0]):
        total = total + got[i, : 16 * few]
    sums[...] = total * (1.0 / math.sqrt(128.0))
    for b in range(few):
        mine = errs[pl.ds(tab[ME, 0] * few + b, 1)]
        grads[b] = sums[pl.ds(b, 16, stride=few)] * mine

    def step(j, carry):
        live = tab[LIVE, j].astype(f32)
        weighted = split(ft[tab[FIRST, j]].astype(f32) * errs[...])
        mats[tab[SLOT, j]] = moved[j] - (rate * live) * dot_lhs(weighted, second[j], ATB)
        return carry

    lax.fori_loop(0, second.shape[0], step, 0, unroll=4)


def call(kernel, outs, n_in, scratch=(), smem=True):
    specs = [pl.BlockSpec(memory_space=pltpu.VMEM)] * n_in
    if smem:
        specs[0] = pl.BlockSpec(memory_space=pltpu.SMEM)
    out_specs = [pl.BlockSpec(memory_space=pltpu.VMEM)] * len(outs)
    return pl.pallas_call(
        kernel,
        out_shape=outs,
        in_specs=specs,
        out_specs=out_specs,
        scratch_shapes=list(scratch),
        compiler_params=pltpu.CompilerParams(vmem_limit_bytes=40 << 20),
    )


def shape(dims, dtype=f32):
    return jax.ShapeDtypeStruct(dims, dtype)


def swap(x, axes):
    return lax.all_to_all(x, axes, split_axis=0, concat_axis=0, tiled=True)


def chunk_of(values):
    padded = jnp.pad(values, (0, 256 - values.shape[0])).reshape(2, 1, 128)
    return jnp.broadcast_to(padded, (2, 4, 128)).reshape(8, 128)


def on_device(fields, labels, pair_first, pair_second, pair_count, pair_mats):
    groups, owners = lax.axis_size(GRP), lax.axis_size(OWN)
    n_x, n_z = lax.axis_size("x"), lax.axis_size("z")
    me = lax.axis_index(GRP)
    samples, per_block, feature = fields.shape
    slots = pair_first.shape[2]
    scale = logit_gain / math.sqrt(groups * owners * slots)
    rate = step_size * scale / (samples * feature)
    few = samples // owners

    table = pair_second[:, 0, :]
    blocks = table // per_block
    served = jnp.sum(jnp.where(blocks == me, table - me * per_block, 0), axis=1)
    mine = lax.dynamic_index_in_dim(blocks, me, 0, keepdims=False)
    picked = mine[:, None] == jnp.arange(slots, dtype=jnp.int32)[None, :]
    slot_ids = jnp.arange(slots, dtype=jnp.int32)[:, None]
    slot_of = jnp.sum(jnp.where(picked, slot_ids, 0), axis=0)
    first_of = jnp.sum(jnp.where(picked, (pair_first[0, 0] - me * per_block)[:, None], 0), axis=0)
    live = (slot_of < pair_count[0, 0]).astype(jnp.int32)
    where_am_i = jnp.full((slots,), lax.axis_index(OWN), jnp.int32)
    tab = jnp.stack([slot_of, first_of, live, served, where_am_i])

    ft = jnp.transpose(fields, (1, 0, 2))
    mats = pair_mats[0, 0]
    targets = chunk_of(labels.astype(f32))

    sent = call(gather_kernel, [shape((slots, samples, feature), bf16)], 2)(tab, ft)[0]
    second = swap(sent, GRP)
    acc = pltpu.VMEM((samples, 128), f32)
    part = call(partial_kernel, [shape((groups, 8, 128))], 4, [acc])(tab, ft, second, mats)[0]
    part = call(sum_kernel, [shape((owners, 8, 128))], 1, smem=False)(swap(part, GRP))[0]
    sums = swap(part, OWN)

    moved, out, dense = call(
        functools.partial(terms_kernel, scale, rate),
        [
            shape(mats.shape),
            shape((slots, samples + 8, feature)),
            shape((n_x, per_block * (samples // n_x) + 8, feature)),
        ],
        6,
        [acc, acc],
    )(tab, ft, second, mats, sums, targets)
    got = swap(out, GRP)
    dense = call(dense_kernel, [shape(dense.shape)], 3)(tab, got, dense)[0]
    got = swap(dense, "x")
    got = call(across_kernel, [shape((n_z, per_block * few + 8, feature))], 1, smem=False)(got)[0]
    got = swap(got, "z")
    logits, grads, mats = call(
        functools.partial(last_kernel, scale, rate),
        [shape((8, 128)), shape((few, per_block, feature)), shape(mats.shape)],
        6,
        [acc, pltpu.VMEM((per_block * few, 128), f32)],
    )(tab, ft, second, moved, got, targets)
    logits = jnp.concatenate([logits[0], logits[4, : samples - 128]])
    return logits, grads, mats[None, None]


def solution(mesh):
    n_grp, n_own = mesh.devices.shape
    sizes = (n_grp // 2, 2, 4, n_own // 4) if n_own % 12 == 0 else (n_grp // 2, 2, 2, n_own // 2)
    split_mesh = Mesh(mesh.devices.reshape(sizes), ("y", "core", "x", "z"))
    in_specs = (
        P(None, GRP, None),
        P(),
        P(GRP, OWN, None),
        P(None, OWN, None),
        P(GRP, OWN),
        P(GRP, OWN, None, None, None),
    )
    out_specs = (P(), P(OWN, GRP, None), P(GRP, OWN, None, None, None))
    return jax.shard_map(
        on_device, mesh=split_mesh, in_specs=in_specs, out_specs=out_specs, check_vma=False
    )
```

```python
import functools
import math

import jax
import jax.numpy as jnp
from jax import lax
from jax.experimental import pallas as pl
from jax.experimental.pallas import tpu as pltpu
from jax.sharding import Mesh
from jax.sharding import PartitionSpec as P

GRP = ("y", "core")
OWN = ("x", "z")
logit_gain = 1.5
step_size = 1000.0
f32 = jnp.float32
bf16 = jnp.bfloat16

SLOT, FIRST, LIVE, SERVED, ME = range(5)


def split(x):
    hi = x.astype(bf16)
    return hi, (x - hi.astype(f32)).astype(bf16)


def dot(a, b, dims):
    return lax.dot_general(a, b, (dims, ((), ())), preferred_element_type=f32)


def dot_rhs(a, pair, dims):
    return dot(a, pair[0], dims) + dot(a, pair[1], dims)


def dot_lhs(pair, b, dims):
    return dot(pair[0], b, dims) + dot(pair[1], b, dims)


AB, ABT, ATB = ((1,), (0,)), ((1,), (1,)), ((0,), (0,))


def row_sums(acc):
    ones = jnp.ones((8, 128), f32)
    exact = functools.partial(
        lax.dot_general,
        dimension_numbers=(ABT, ((), ())),
        precision=lax.Precision.HIGHEST,
        preferred_element_type=f32,
    )
    low = exact(ones, acc[:128])
    rest = acc[128:]
    high = exact(ones, jnp.concatenate([rest, jnp.zeros((256 - acc.shape[0], 128), f32)], axis=0))
    rows = lax.broadcasted_iota(jnp.int32, (8, 128), 0)
    return jnp.where(rows < 4, low, high)


def spread(chunk, samples):
    low = jnp.transpose(jnp.broadcast_to(chunk[0:1], (128, 128)))
    high = jnp.transpose(jnp.broadcast_to(chunk[4:5], (128, 128)))
    return jnp.concatenate([low, high[: samples - 128]], axis=0)


def gather_kernel(tab, ft, out):
    @pl.loop(0, out.shape[0])
    def _(j):
        out[j] = ft[tab[SERVED, j]]


def partial_kernel(tab, ft, second, mats, out, acc):
    acc[...] = jnp.zeros_like(acc)

    def step(j, carry):
        live = tab[LIVE, j].astype(f32)
        mixed = dot_rhs(ft[tab[FIRST, j]], split(mats[tab[SLOT, j]] * live), AB)
        acc[...] += mixed * second[j].astype(f32)
        return carry

    lax.fori_loop(0, second.shape[0], step, 0, unroll=4)
    chunk = row_sums(acc[...] * (1.0 / 128.0))
    for i in range(out.shape[0]):
        out[i] = chunk


def sum_kernel(parts, out):
    total = parts[0]
    for i in range(1, parts.shape[0]):
        total = total + parts[i]
    for i in range(out.shape[0]):
        out[i] = total


def total_of(parts, lo):
    total = parts[0, lo : lo + 8]
    for i in range(1, parts.shape[0]):
        total = total + parts[i, lo : lo + 8]
    return total


LEVELS = 32000.0
OCTAVE = 64.0


def exponent(peak):
    return jnp.ceil(OCTAVE * jnp.log2(jnp.maximum(peak, 1e-30)))


def scale_of(k):
    return jnp.exp2(k * (1.0 / OCTAVE))


def whole(x):
    return jnp.round(x).astype(jnp.int32).astype(jnp.int16)


def real(x):
    return x.astype(jnp.int32).astype(f32)


def peaks(x):
    return jnp.max(jnp.abs(x), axis=1, keepdims=True)


def iota(dims, axis):
    return lax.broadcasted_iota(jnp.int32, dims, axis)


def rows_of(named):
    rows = iota((16, 128), 0)
    out = jnp.zeros((16, 128), f32)
    for r, value in named.items():
        out = jnp.where(rows == r, value, out)
    return out


def digits(low, high, at):
    k = exponent(jnp.maximum(peaks(low), peaks(high)))
    up = LEVELS * scale_of(-k)
    a, b = low * up, high * up
    named = {at: jnp.round(a), at + 1: jnp.round(b)}
    named[at + 2] = (a - named[at]) * LEVELS
    named[at + 3] = (b - named[at + 1]) * LEVELS
    named[at + 4] = jnp.broadcast_to(k, (1, 128))
    return named


def undigit(tile, at):
    s = scale_of(tile[at + 4 : at + 5]) * (1.0 / LEVELS)
    low = s * (tile[at : at + 1] + tile[at + 2 : at + 3] * (1.0 / LEVELS))
    high = s * (tile[at + 1 : at + 2] + tile[at + 3 : at + 4] * (1.0 / LEVELS))
    return low, high


def upright(rows, height):
    tall = jnp.concatenate(rows + [jnp.zeros((128 - len(rows), 128), f32)], axis=0)
    return jnp.transpose(tall)[:height]


def terms_kernel(
    scale, rate, tab, ft, second, mats, sums, labels, moved, out, dense, acc, errs, stash, tops
):
    samples = second.shape[1]
    n_x, rows = dense.shape[0], samples // dense.shape[0]
    errors = jax.nn.sigmoid(scale * total_of(sums, 0)) - labels[...]
    errs[...] = spread(errors, samples)
    acc[...] = jnp.zeros_like(acc)
    dense[...] = jnp.zeros_like(dense)
    tops[...] = jnp.zeros_like(tops)
    lanes = iota((samples, 128), 1)

    def step(j, carry):
        live = tab[LIVE, j].astype(f32)
        slot, first = tab[SLOT, j], tab[FIRST, j]
        va, vb = ft[first], second[j]
        gradient = dot_lhs(split(va.astype(f32) * errs[...]), vb, ATB)
        updated = mats[slot] - (rate * live) * gradient
        moved[j] = updated
        pair = split(updated * live)
        mixed = dot_rhs(va, pair, AB)
        acc[...] += mixed * vb.astype(f32)
        stash[j] = mixed
        tops[...] = jnp.where(lanes == j, peaks(mixed), tops[...])
        toward = dot_rhs(vb, pair, ABT)
        at = pl.ds(pl.multiple_of(first * rows, 8), rows)
        for i in range(n_x):
            dense[i, at] += toward[i * rows : (i + 1) * rows]
        return carry

    lax.fori_loop(0, second.shape[0], step, 0, unroll=2)
    k = exponent(tops[...])
    up = LEVELS * scale_of(-k)
    low = jnp.transpose(k[:128])
    high = jnp.transpose(
        jnp.concatenate([k[128:], jnp.zeros((256 - samples, 128), f32)], axis=0)
    )
    chunk = row_sums(acc[...] * (1.0 / 128.0))
    tile = rows_of(digits(chunk[0:1], chunk[4:5], 0))
    rows = iota((16, 128), 0)
    for j in range(out.shape[0]):
        out[j, 0:samples] = whole(stash[j] * up[:, j : j + 1])
        mine = jnp.where(rows == 6, high[j : j + 1], tile)
        out[j, samples : samples + 16] = whole(jnp.where(rows == 5, low[j : j + 1], mine))


def dense_kernel(tab, got, dense_in, out, dense):
    samples = got.shape[1] - 16
    n_x, rows = dense.shape[0], samples // dense.shape[0]
    size = dense.shape[1]
    parts = size // 128
    tiles = [real(got[j, samples : samples + 16]) for j in range(got.shape[0])]
    low = upright([t[5:6] for t in tiles], 128)
    high = upright([t[6:7] for t in tiles], samples - 128)
    down = scale_of(jnp.concatenate([low, high], axis=0)) * (1.0 / LEVELS)
    dense[...] = dense_in[...]
    sums = [undigit(t, 0) for t in tiles]
    total = sums[0]
    for j in range(got.shape[0]):
        at = pl.ds(pl.multiple_of(tab[SERVED, j] * rows, 8), rows)
        value = real(got[j, 0:samples]) * down[:, j : j + 1]
        for i in range(n_x):
            dense[i, at] += value[i * rows : (i + 1) * rows]
        if j:
            total = (total[0] + sums[j][0], total[1] + sums[j][1])

    lanes = iota((128, 128), 1)
    tops = jnp.zeros((128, 128), f32)
    for i in range(n_x):
        for t in range(parts):
            top = peaks(dense[i, t * 128 : (t + 1) * 128])
            tops = jnp.where(lanes == i * parts + t, top, tops)
    k = exponent(tops)
    up = LEVELS * scale_of(-k)
    lying = jnp.transpose(k)
    common = digits(total[0], total[1], parts)
    for i in range(n_x):
        named = dict(common)
        for t in range(parts):
            lane = i * parts + t
            part = dense[i, t * 128 : (t + 1) * 128]
            out[i, t * 128 : (t + 1) * 128] = whole(part * up[:, lane : lane + 1])
            named[t] = lying[lane : lane + 1]
        out[i, size : size + 16] = whole(rows_of(named))


def across_kernel(got, out, sums, parted):
    n_z, wide = out.shape[0], out.shape[1] - 16
    few = wide // 16
    rows = n_z * few
    size = 16 * rows
    parts = size // 128
    tiles = [real(got[i, size : size + 16]) for i in range(got.shape[0])]
    exps = upright([t[r : r + 1] for t in tiles for r in range(parts)], 128)
    down = scale_of(exps) * (1.0 / LEVELS)
    for t in range(parts):
        total = real(got[0, t * 128 : (t + 1) * 128]) * down[:, t : t + 1]
        for i in range(1, got.shape[0]):
            lane = i * parts + t
            total = total + real(got[i, t * 128 : (t + 1) * 128]) * down[:, lane : lane + 1]
        sums[t * 128 : (t + 1) * 128] = total
    pair = undigit(tiles[0], parts)
    for t in tiles[1:]:
        more = undigit(t, parts)
        pair = (pair[0] + more[0], pair[1] + more[1])
    for f in range(16):
        for z in range(n_z):
            start = f * rows + z * few
            parted[z, f * few : (f + 1) * few] = sums[start : start + few]
    lanes = iota((wide, 128), 1)
    tops = jnp.zeros((wide, 128), f32)
    for z in range(n_z):
        tops = jnp.where(lanes == z, peaks(parted[z]), tops)
    k = exponent(tops)
    up = LEVELS * scale_of(-k)
    if wide < 128:
        k = jnp.concatenate([k, jnp.zeros((128 - wide, 128), f32)], axis=0)
    lying = [jnp.transpose(k[n * 128 : (n + 1) * 128]) for n in range(k.shape[0] // 128)]
    common = digits(pair[0], pair[1], len(lying))
    for z in range(n_z):
        out[z, 0:wide] = whole(parted[z] * up[:, z : z + 1])
        named = dict(common)
        for n, part in enumerate(lying):
            named[n] = part[z : z + 1]
        out[z, wide : wide + 16] = whole(rows_of(named))


def last_kernel(
    scale, rate, tab, ft, second, moved, got, labels, logits, grads, mats, errs, sums
):
    samples = second.shape[1]
    few = grads.shape[0]
    wide = 16 * few
    tiles = [real(got[i, wide : wide + 16]) for i in range(got.shape[0])]
    high = -(-wide // 128)
    exps = [upright([t[n : n + 1] for t in tiles], min(wide, 128)) for n in range(high)]
    down = scale_of(jnp.concatenate(exps, axis=0)) * (1.0 / LEVELS)
    pair = undigit(tiles[0], high)
    for t in tiles[1:]:
        more = undigit(t, high)
        pair = (pair[0] + more[0], pair[1] + more[1])
    value = scale * jnp.where(iota((8, 128), 0) < 4, pair[0], pair[1])
    logits[...] = value
    errs[...] = spread(jax.nn.sigmoid(value) - labels[...], samples)
    total = real(got[0, 0:wide]) * down[:, 0:1]
    for i in range(1, got.shape[0]):
        total = total + real(got[i, 0:wide]) * down[:, i : i + 1]
    sums[...] = total * (1.0 / math.sqrt(128.0))
    for b in range(few):
        mine = errs[pl.ds(tab[ME, 0] * few + b, 1)]
        grads[b] = sums[pl.ds(b, 16, stride=few)] * mine

    def step(j, carry):
        live = tab[LIVE, j].astype(f32)
        weighted = split(ft[tab[FIRST, j]].astype(f32) * errs[...])
        mats[tab[SLOT, j]] = moved[j] - (rate * live) * dot_lhs(weighted, second[j], ATB)
        return carry

    lax.fori_loop(0, second.shape[0], step, 0, unroll=4)


def call(kernel, outs, n_in, scratch=(), smem=True):
    specs = [pl.BlockSpec(memory_space=pltpu.VMEM)] * n_in
    if smem:
        specs[0] = pl.BlockSpec(memory_space=pltpu.SMEM)
    out_specs = [pl.BlockSpec(memory_space=pltpu.VMEM)] * len(outs)
    return pl.pallas_call(
        kernel,
        out_shape=outs,
        in_specs=specs,
        out_specs=out_specs,
        scratch_shapes=list(scratch),
        compiler_params=pltpu.CompilerParams(vmem_limit_bytes=40 << 20),
    )


def shape(dims, dtype=f32):
    return jax.ShapeDtypeStruct(dims, dtype)


def swap(x, axes):
    return lax.all_to_all(x, axes, split_axis=0, concat_axis=0, tiled=True)


def chunk_of(values):
    padded = jnp.pad(values, (0, 256 - values.shape[0])).reshape(2, 1, 128)
    return jnp.broadcast_to(padded, (2, 4, 128)).reshape(8, 128)


def on_device(fields, labels, pair_first, pair_second, pair_count, pair_mats):
    groups, owners = lax.axis_size(GRP), lax.axis_size(OWN)
    n_x, n_z = lax.axis_size("x"), lax.axis_size("z")
    me = lax.axis_index(GRP)
    samples, per_block, feature = fields.shape
    slots = pair_first.shape[2]
    scale = logit_gain / math.sqrt(groups * owners * slots)
    rate = step_size * scale / (samples * feature)
    few = samples // owners

    table = pair_second[:, 0, :]
    blocks = table // per_block
    served = jnp.sum(jnp.where(blocks == me, table - me * per_block, 0), axis=1)
    mine = lax.dynamic_index_in_dim(blocks, me, 0, keepdims=False)
    picked = mine[:, None] == jnp.arange(slots, dtype=jnp.int32)[None, :]
    slot_ids = jnp.arange(slots, dtype=jnp.int32)[:, None]
    slot_of = jnp.sum(jnp.where(picked, slot_ids, 0), axis=0)
    first_of = jnp.sum(jnp.where(picked, (pair_first[0, 0] - me * per_block)[:, None], 0), axis=0)
    live = (slot_of < pair_count[0, 0]).astype(jnp.int32)
    where_am_i = jnp.full((slots,), lax.axis_index(OWN), jnp.int32)
    tab = jnp.stack([slot_of, first_of, live, served, where_am_i])

    ft = jnp.transpose(fields, (1, 0, 2))
    mats = pair_mats[0, 0]
    targets = chunk_of(labels.astype(f32))

    sent = call(gather_kernel, [shape((slots, samples, feature), bf16)], 2)(tab, ft)[0]
    second = swap(sent, GRP)
    acc = pltpu.VMEM((samples, 128), f32)
    part = call(partial_kernel, [shape((groups, 8, 128))], 4, [acc])(tab, ft, second, mats)[0]
    part = call(sum_kernel, [shape((owners, 8, 128))], 1, smem=False)(swap(part, GRP))[0]
    sums = swap(part, OWN)

    size, wide = per_block * (samples // n_x), per_block * few
    moved, out, dense = call(
        functools.partial(terms_kernel, scale, rate),
        [
            shape(mats.shape),
            shape((slots, samples + 16, feature), jnp.int16),
            shape((n_x, size, feature)),
        ],
        6,
        [acc, acc, pltpu.VMEM((slots, samples, feature), f32), acc],
    )(tab, ft, second, mats, sums, targets)
    got = swap(out, GRP)
    out = [shape((n_x, size + 16, feature), jnp.int16)]
    got = call(dense_kernel, out, 3, [pltpu.VMEM((n_x, size, feature), f32)])(tab, got, dense)[0]
    got = swap(got, "x")
    out = [shape((n_z, wide + 16, feature), jnp.int16)]
    room = [pltpu.VMEM((size, feature), f32), pltpu.VMEM((n_z, wide, feature), f32)]
    got = call(across_kernel, out, 1, room, smem=False)(got)[0]
    got = swap(got, "z")
    logits, grads, mats = call(
        functools.partial(last_kernel, scale, rate),
        [shape((8, 128)), shape((few, per_block, feature)), shape(mats.shape)],
        6,
        [acc, pltpu.VMEM((per_block * few, 128), f32)],
    )(tab, ft, second, moved, got, targets)
    logits = jnp.concatenate([logits[0], logits[4, : samples - 128]])
    return logits, grads, mats[None, None]


def solution(mesh):
    n_grp, n_own = mesh.devices.shape
    sizes = (n_grp // 2, 2, 4, n_own // 4)
    split_mesh = Mesh(mesh.devices.reshape(sizes), ("y", "core", "x", "z"))
    in_specs = (
        P(None, GRP, None),
        P(),
        P(GRP, OWN, None),
        P(None, OWN, None),
        P(GRP, OWN),
        P(GRP, OWN, None, None, None),
    )
    out_specs = (P(), P(OWN, GRP, None), P(GRP, OWN, None, None, None))
    return jax.shard_map(
        on_device, mesh=split_mesh, in_specs=in_specs, out_specs=out_specs, check_vma=False
    )
```

```python
import functools
import math

import jax
import jax.numpy as jnp
from jax import lax
from jax.experimental import pallas as pl
from jax.experimental.pallas import tpu as pltpu
from jax.sharding import Mesh
from jax.sharding import PartitionSpec as P

GRP = ("y", "core")
OWN = ("x", "z")
logit_gain = 1.5
step_size = 1000.0
f32 = jnp.float32
bf16 = jnp.bfloat16

SLOT, FIRST, LIVE, SERVED, ME = range(5)


def split(x):
    hi = x.astype(bf16)
    return hi, (x - hi.astype(f32)).astype(bf16)


def dot(a, b, dims):
    return lax.dot_general(a, b, (dims, ((), ())), preferred_element_type=f32)


def dot_rhs(a, pair, dims):
    return dot(a, pair[0], dims) + dot(a, pair[1], dims)


def dot_lhs(pair, b, dims):
    return dot(pair[0], b, dims) + dot(pair[1], b, dims)


AB, ABT, ATB = ((1,), (0,)), ((1,), (1,)), ((0,), (0,))


def row_sums(acc):
    ones = jnp.ones((8, 128), f32)
    exact = functools.partial(
        lax.dot_general,
        dimension_numbers=(ABT, ((), ())),
        precision=lax.Precision.HIGHEST,
        preferred_element_type=f32,
    )
    low = exact(ones, acc[:128])
    rest = acc[128:]
    high = exact(ones, jnp.concatenate([rest, jnp.zeros((256 - acc.shape[0], 128), f32)], axis=0))
    return jnp.concatenate([low[0:1], high[0:1]], axis=0)


def spread(chunk, samples):
    low = jnp.transpose(jnp.broadcast_to(chunk[0:1], (128, 128)))
    high = jnp.transpose(jnp.broadcast_to(chunk[1:2], (128, 128)))
    return jnp.concatenate([low, high[: samples - 128]], axis=0)


def gather_kernel(tab, ft, out):
    @pl.loop(0, out.shape[0])
    def _(j):
        out[j] = ft[tab[SERVED, j]]


def partial_kernel(tab, ft, second, mats, out, acc):
    acc[...] = jnp.zeros_like(acc)

    def step(j, carry):
        live = tab[LIVE, j].astype(f32)
        mixed = dot_rhs(ft[tab[FIRST, j]], split(mats[tab[SLOT, j]] * live), AB)
        acc[...] += mixed * second[j].astype(f32)
        return carry

    lax.fori_loop(0, second.shape[0], step, 0, unroll=4)
    chunk = row_sums(acc[...] * (1.0 / 128.0))
    for i in range(out.shape[0]):
        out[i] = chunk


def sum_kernel(parts, out):
    total = total_of(parts)
    for i in range(out.shape[0]):
        out[i] = total


def total_of(parts):
    total = parts[0]
    for i in range(1, parts.shape[0]):
        total = total + parts[i]
    return total


LEVELS = 32000.0
OCTAVE = 64.0


def exponent(peak):
    return jnp.ceil(OCTAVE * jnp.log2(jnp.maximum(peak, 1e-30)))


def scale_of(k):
    return jnp.exp2(k * (1.0 / OCTAVE))


def whole(x):
    return jnp.round(x).astype(jnp.int32).astype(jnp.int16)


def real(x):
    return x.astype(jnp.int32).astype(f32)


def peaks(x):
    return jnp.max(jnp.abs(x), axis=1, keepdims=True)


def iota(dims, axis):
    return lax.broadcasted_iota(jnp.int32, dims, axis)


def rows_of(named):
    rows = iota((16, 128), 0)
    out = jnp.zeros((16, 128), f32)
    for r, value in named.items():
        out = jnp.where(rows == r, value, out)
    return out


def digits(low, high, at):
    k = exponent(jnp.maximum(peaks(low), peaks(high)))
    up = LEVELS * scale_of(-k)
    a, b = low * up, high * up
    named = {at: jnp.round(a), at + 1: jnp.round(b)}
    named[at + 2] = (a - named[at]) * LEVELS
    named[at + 3] = (b - named[at + 1]) * LEVELS
    named[at + 4] = jnp.broadcast_to(k, (1, 128))
    return named


def undigit(tile, at):
    s = scale_of(tile[at + 4 : at + 5]) * (1.0 / LEVELS)
    low = s * (tile[at : at + 1] + tile[at + 2 : at + 3] * (1.0 / LEVELS))
    high = s * (tile[at + 1 : at + 2] + tile[at + 3 : at + 4] * (1.0 / LEVELS))
    return low, high


def upright(rows, height):
    tall = jnp.concatenate(rows + [jnp.zeros((128 - len(rows), 128), f32)], axis=0)
    return jnp.transpose(tall)[:height]


def terms_kernel(
    scale, rate, tab, ft, second, mats, sums, labels, moved, out, dense, acc, errs, stash, tops
):
    samples = second.shape[1]
    n_x, rows = dense.shape[0], samples // dense.shape[0]
    errors = jax.nn.sigmoid(scale * total_of(sums)) - labels[...]
    errs[...] = spread(errors, samples)
    acc[...] = jnp.zeros_like(acc)
    dense[...] = jnp.zeros_like(dense)
    tops[...] = jnp.zeros_like(tops)
    lanes = iota((samples, 128), 1)

    def step(j, carry):
        live = tab[LIVE, j].astype(f32)
        slot, first = tab[SLOT, j], tab[FIRST, j]
        va, vb = ft[first], second[j]
        gradient = dot_lhs(split(va.astype(f32) * errs[...]), vb, ATB)
        updated = mats[slot] - (rate * live) * gradient
        moved[j] = updated
        pair = split(updated * live)
        mixed = dot_rhs(va, pair, AB)
        acc[...] += mixed * vb.astype(f32)
        stash[j] = mixed
        tops[...] = jnp.where(lanes == j, peaks(mixed), tops[...])
        toward = dot_rhs(vb, pair, ABT)
        at = pl.ds(pl.multiple_of(first * rows, 8), rows)
        for i in range(n_x):
            dense[i, at] += toward[i * rows : (i + 1) * rows]
        return carry

    lax.fori_loop(0, second.shape[0], step, 0, unroll=2)
    k = exponent(tops[...])
    up = LEVELS * scale_of(-k)
    low = jnp.transpose(k[:128])
    high = jnp.transpose(
        jnp.concatenate([k[128:], jnp.zeros((256 - samples, 128), f32)], axis=0)
    )
    chunk = row_sums(acc[...] * (1.0 / 128.0))
    tile = rows_of(digits(chunk[0:1], chunk[1:2], 0))
    rows = iota((16, 128), 0)
    for j in range(out.shape[0]):
        out[j, 0:samples] = whole(stash[j] * up[:, j : j + 1])
        mine = jnp.where(rows == 6, high[j : j + 1], tile)
        out[j, samples : samples + 16] = whole(jnp.where(rows == 5, low[j : j + 1], mine))


def dense_kernel(tab, got, dense_in, out, dense):
    samples = got.shape[1] - 16
    n_x, rows = dense.shape[0], samples // dense.shape[0]
    size = dense.shape[1]
    parts = size // 128
    tiles = [real(got[j, samples : samples + 16]) for j in range(got.shape[0])]
    low = upright([t[5:6] for t in tiles], 128)
    high = upright([t[6:7] for t in tiles], samples - 128)
    down = scale_of(jnp.concatenate([low, high], axis=0)) * (1.0 / LEVELS)
    dense[...] = dense_in[...]
    sums = [undigit(t, 0) for t in tiles]
    total = sums[0]
    for j in range(got.shape[0]):
        at = pl.ds(pl.multiple_of(tab[SERVED, j] * rows, 8), rows)
        value = real(got[j, 0:samples]) * down[:, j : j + 1]
        for i in range(n_x):
            dense[i, at] += value[i * rows : (i + 1) * rows]
        if j:
            total = (total[0] + sums[j][0], total[1] + sums[j][1])

    lanes = iota((128, 128), 1)
    tops = jnp.zeros((128, 128), f32)
    for i in range(n_x):
        for t in range(parts):
            top = peaks(dense[i, t * 128 : (t + 1) * 128])
            tops = jnp.where(lanes == i * parts + t, top, tops)
    k = exponent(tops)
    up = LEVELS * scale_of(-k)
    lying = jnp.transpose(k)
    common = digits(total[0], total[1], parts)
    for i in range(n_x):
        named = dict(common)
        for t in range(parts):
            lane = i * parts + t
            part = dense[i, t * 128 : (t + 1) * 128]
            out[i, t * 128 : (t + 1) * 128] = whole(part * up[:, lane : lane + 1])
            named[t] = lying[lane : lane + 1]
        out[i, size : size + 16] = whole(rows_of(named))


def across_kernel(got, out, sums, parted):
    n_z, wide = out.shape[0], out.shape[1] - 16
    few = wide // 16
    rows = n_z * few
    size = 16 * rows
    parts = size // 128
    tiles = [real(got[i, size : size + 16]) for i in range(got.shape[0])]
    exps = upright([t[r : r + 1] for t in tiles for r in range(parts)], 128)
    down = scale_of(exps) * (1.0 / LEVELS)
    for t in range(parts):
        total = real(got[0, t * 128 : (t + 1) * 128]) * down[:, t : t + 1]
        for i in range(1, got.shape[0]):
            lane = i * parts + t
            total = total + real(got[i, t * 128 : (t + 1) * 128]) * down[:, lane : lane + 1]
        sums[t * 128 : (t + 1) * 128] = total
    pair = undigit(tiles[0], parts)
    for t in tiles[1:]:
        more = undigit(t, parts)
        pair = (pair[0] + more[0], pair[1] + more[1])
    for f in range(16):
        for z in range(n_z):
            start = f * rows + z * few
            parted[z, f * few : (f + 1) * few] = sums[start : start + few]
    lanes = iota((wide, 128), 1)
    tops = jnp.zeros((wide, 128), f32)
    for z in range(n_z):
        tops = jnp.where(lanes == z, peaks(parted[z]), tops)
    k = exponent(tops)
    up = LEVELS * scale_of(-k)
    if wide < 128:
        k = jnp.concatenate([k, jnp.zeros((128 - wide, 128), f32)], axis=0)
    lying = [jnp.transpose(k[n * 128 : (n + 1) * 128]) for n in range(k.shape[0] // 128)]
    common = digits(pair[0], pair[1], len(lying))
    for z in range(n_z):
        out[z, 0:wide] = whole(parted[z] * up[:, z : z + 1])
        named = dict(common)
        for n, part in enumerate(lying):
            named[n] = part[z : z + 1]
        out[z, wide : wide + 16] = whole(rows_of(named))


def last_kernel(
    scale, rate, tab, ft, second, moved, got, labels, logits, grads, mats, errs, sums
):
    samples = second.shape[1]
    few = grads.shape[0]
    wide = 16 * few
    tiles = [real(got[i, wide : wide + 16]) for i in range(got.shape[0])]
    high = -(-wide // 128)
    exps = [upright([t[n : n + 1] for t in tiles], min(wide, 128)) for n in range(high)]
    down = scale_of(jnp.concatenate(exps, axis=0)) * (1.0 / LEVELS)
    pair = undigit(tiles[0], high)
    for t in tiles[1:]:
        more = undigit(t, high)
        pair = (pair[0] + more[0], pair[1] + more[1])
    value = scale * jnp.concatenate(pair, axis=0)
    logits[...] = value
    errs[...] = spread(jax.nn.sigmoid(value) - labels[...], samples)
    total = real(got[0, 0:wide]) * down[:, 0:1]
    for i in range(1, got.shape[0]):
        total = total + real(got[i, 0:wide]) * down[:, i : i + 1]
    sums[...] = total * (1.0 / math.sqrt(128.0))
    for b in range(few):
        mine = errs[pl.ds(tab[ME, 0] * few + b, 1)]
        grads[b] = sums[pl.ds(b, 16, stride=few)] * mine

    def step(j, carry):
        live = tab[LIVE, j].astype(f32)
        weighted = split(ft[tab[FIRST, j]].astype(f32) * errs[...])
        mats[tab[SLOT, j]] = moved[j] - (rate * live) * dot_lhs(weighted, second[j], ATB)
        return carry

    lax.fori_loop(0, second.shape[0], step, 0, unroll=4)


def call(kernel, outs, n_in, scratch=(), smem=True):
    specs = [pl.BlockSpec(memory_space=pltpu.VMEM)] * n_in
    if smem:
        specs[0] = pl.BlockSpec(memory_space=pltpu.SMEM)
    out_specs = [pl.BlockSpec(memory_space=pltpu.VMEM)] * len(outs)
    return pl.pallas_call(
        kernel,
        out_shape=outs,
        in_specs=specs,
        out_specs=out_specs,
        scratch_shapes=list(scratch),
        compiler_params=pltpu.CompilerParams(vmem_limit_bytes=40 << 20),
    )


def shape(dims, dtype=f32):
    return jax.ShapeDtypeStruct(dims, dtype)


def swap(x, axes):
    return lax.all_to_all(x, axes, split_axis=0, concat_axis=0, tiled=True)


def on_device(fields, labels, pair_first, pair_second, pair_count, pair_mats):
    groups, owners = lax.axis_size(GRP), lax.axis_size(OWN)
    n_x, n_z = lax.axis_size("x"), lax.axis_size("z")
    me = lax.axis_index(GRP)
    samples, per_block, feature = fields.shape
    slots = pair_first.shape[2]
    scale = logit_gain / math.sqrt(groups * owners * slots)
    rate = step_size * scale / (samples * feature)
    few = samples // owners

    table = pair_second[:, 0, :]
    blocks = table // per_block
    served = jnp.sum(jnp.where(blocks == me, table - me * per_block, 0), axis=1)
    mine = lax.dynamic_index_in_dim(blocks, me, 0, keepdims=False)
    picked = mine[:, None] == jnp.arange(slots, dtype=jnp.int32)[None, :]
    slot_ids = jnp.arange(slots, dtype=jnp.int32)[:, None]
    slot_of = jnp.sum(jnp.where(picked, slot_ids, 0), axis=0)
    first_of = jnp.sum(jnp.where(picked, (pair_first[0, 0] - me * per_block)[:, None], 0), axis=0)
    live = (slot_of < pair_count[0, 0]).astype(jnp.int32)
    where_am_i = jnp.full((slots,), lax.axis_index(OWN), jnp.int32)
    tab = jnp.stack([slot_of, first_of, live, served, where_am_i])

    ft = jnp.transpose(fields, (1, 0, 2))
    mats = pair_mats[0, 0]
    targets = jnp.pad(labels.astype(f32), (0, 256 - samples)).reshape(2, 128)

    sent = call(gather_kernel, [shape((slots, samples, feature), bf16)], 2)(tab, ft)[0]
    second = swap(sent, GRP)
    acc = pltpu.VMEM((samples, 128), f32)
    part = call(partial_kernel, [shape((groups * n_x, 2, 128))], 4, [acc])(tab, ft, second, mats)[0]
    part = call(sum_kernel, [shape((n_z, 2, 128))], 1, smem=False)(swap(part, GRP + ("x",)))[0]
    sums = swap(part, "z")

    size, wide = per_block * (samples // n_x), per_block * few
    moved, out, dense = call(
        functools.partial(terms_kernel, scale, rate),
        [
            shape(mats.shape),
            shape((slots, samples + 16, feature), jnp.int16),
            shape((n_x, size, feature)),
        ],
        6,
        [acc, acc, pltpu.VMEM((slots, samples, feature), f32), acc],
    )(tab, ft, second, mats, sums, targets)
    got = swap(out, GRP)
    out = [shape((n_x, size + 16, feature), jnp.int16)]
    got = call(dense_kernel, out, 3, [pltpu.VMEM((n_x, size, feature), f32)])(tab, got, dense)[0]
    got = swap(got, "x")
    out = [shape((n_z, wide + 16, feature), jnp.int16)]
    room = [pltpu.VMEM((size, feature), f32), pltpu.VMEM((n_z, wide, feature), f32)]
    got = call(across_kernel, out, 1, room, smem=False)(got)[0]
    got = swap(got, "z")
    logits, grads, mats = call(
        functools.partial(last_kernel, scale, rate),
        [shape((2, 128)), shape((few, per_block, feature)), shape(mats.shape)],
        6,
        [acc, pltpu.VMEM((per_block * few, 128), f32)],
    )(tab, ft, second, moved, got, targets)
    return logits.reshape(256)[:samples], grads, mats[None, None]


def solution(mesh):
    n_grp, n_own = mesh.devices.shape
    sizes = (n_grp // 2, 2, 4, n_own // 4)
    split_mesh = Mesh(mesh.devices.reshape(sizes), ("y", "core", "x", "z"))
    in_specs = (
        P(None, GRP, None),
        P(),
        P(GRP, OWN, None),
        P(None, OWN, None),
        P(GRP, OWN),
        P(GRP, OWN, None, None, None),
    )
    out_specs = (P(), P(OWN, GRP, None), P(GRP, OWN, None, None, None))
    return jax.shard_map(
        on_device, mesh=split_mesh, in_specs=in_specs, out_specs=out_specs, check_vma=False
    )
```

```python
import functools
import math

import jax
import jax.numpy as jnp
from jax import lax
from jax.experimental import pallas as pl
from jax.experimental.pallas import tpu as pltpu
from jax.sharding import Mesh
from jax.sharding import PartitionSpec as P

GRP = ("y", "core")
OWN = ("x", "z")
logit_gain = 1.5
step_size = 1000.0
f32 = jnp.float32
bf16 = jnp.bfloat16

SLOT, FIRST, LIVE, SERVED, MY_OWN, MY_GRP, MY_X = range(7)
SPARE = 64


def split(x):
    hi = x.astype(bf16)
    return hi, (x - hi.astype(f32)).astype(bf16)


def dot(a, b, dims):
    return lax.dot_general(a, b, (dims, ((), ())), preferred_element_type=f32)


def dot_rhs(a, pair, dims):
    return dot(a, pair[0], dims) + dot(a, pair[1], dims)


def dot_lhs(pair, b, dims):
    return dot(pair[0], b, dims) + dot(pair[1], b, dims)


AB, ABT, ATB = ((1,), (0,)), ((1,), (1,)), ((0,), (0,))


def row_sums(acc):
    ones = jnp.ones((8, 128), f32)
    exact = functools.partial(
        lax.dot_general,
        dimension_numbers=(ABT, ((), ())),
        precision=lax.Precision.HIGHEST,
        preferred_element_type=f32,
    )
    low = exact(ones, acc[:128])
    rest = acc[128:]
    high = exact(ones, jnp.concatenate([rest, jnp.zeros((256 - acc.shape[0], 128), f32)], axis=0))
    return jnp.concatenate([low[0:1], high[0:1]], axis=0)


def spread(chunk, samples):
    low = jnp.transpose(jnp.broadcast_to(chunk[0:1], (128, 128)))
    high = jnp.transpose(jnp.broadcast_to(chunk[1:2], (128, 128)))
    return jnp.concatenate([low, high[: samples - 128]], axis=0)


def gather_kernel(tab, ft, out):
    @pl.loop(0, out.shape[0])
    def _(j):
        out[j] = ft[tab[SERVED, j]]


def partial_kernel(tab, ft, second, mats, out, acc):
    acc[...] = jnp.zeros_like(acc)

    def step(j, carry):
        live = tab[LIVE, j].astype(f32)
        mixed = dot_rhs(ft[tab[FIRST, j]], split(mats[tab[SLOT, j]] * live), AB)
        acc[...] += mixed * second[j].astype(f32)
        return carry

    lax.fori_loop(0, second.shape[0], step, 0, unroll=4)
    chunk = row_sums(acc[...] * (1.0 / 128.0))
    lanes = iota((2, 128), 1) + 128 * (1 - iota((2, 128), 0))
    for j in range(second.shape[0]):
        chunk = jnp.where(lanes == SPARE + j, tab[SERVED, j].astype(f32), chunk)
    for i in range(out.shape[0]):
        out[i] = chunk


def sum_kernel(tab, parts, out, served):
    total = total_of(parts)
    for i in range(out.shape[0]):
        out[i] = total
    n_x = served.shape[0]
    near = parts[pl.ds(tab[MY_GRP, 0] * n_x, n_x)]
    lanes = iota((1, 128), 1)
    mine = (lanes >= SPARE) & (lanes < SPARE + 16)
    for i in range(n_x):
        served[i : i + 1] = jnp.where(mine, near[i, 1:2], 0.0).astype(jnp.int32)


def total_of(parts):
    total = parts[0]
    for i in range(1, parts.shape[0]):
        total = total + parts[i]
    return total


LEVELS = 32000.0
OCTAVE = 64.0


def exponent(peak):
    return jnp.ceil(OCTAVE * jnp.log2(jnp.maximum(peak, 1e-30)))


def scale_of(k):
    return jnp.exp2(k * (1.0 / OCTAVE))


def whole(x):
    return jnp.round(x).astype(jnp.int32).astype(jnp.int16)


def real(x):
    return x.astype(jnp.int32).astype(f32)


def peaks(x):
    return jnp.max(jnp.abs(x), axis=1, keepdims=True)


def iota(dims, axis):
    return lax.broadcasted_iota(jnp.int32, dims, axis)


def tile_of(height, pieces):
    used = sum(p.shape[0] for p in pieces)
    return jnp.concatenate(pieces + [jnp.zeros((height - used, 128), f32)], axis=0)


def digits(pair):
    k = exponent(jnp.max(peaks(pair), axis=0, keepdims=True))
    wide = pair * (LEVELS * scale_of(-k))
    high = jnp.round(wide)
    return [high, (wide - high) * LEVELS, jnp.broadcast_to(k, (1, 128))]


def undigit(tile, at):
    s = scale_of(tile[at + 4 : at + 5]) * (1.0 / LEVELS)
    return s * (tile[at : at + 2] + tile[at + 2 : at + 4] * (1.0 / LEVELS))


def undigits(tiles, at):
    total = undigit(tiles[0], at)
    for t in tiles[1:]:
        total = total + undigit(t, at)
    return total


def upright(rows, height):
    tall = jnp.concatenate(rows + [jnp.zeros((128 - len(rows), 128), f32)], axis=0)
    return jnp.transpose(tall)[:height]


def terms_kernel(
    scale, rate, tab, ft, second, mats, sums, labels,
    moved, out, own, to_1, to_2, to_3, acc, errs, stash, tops, dense,
):
    samples = second.shape[1]
    n_x, size = dense.shape[0], dense.shape[1]
    rows, parts = samples // n_x, size // 128
    errors = jax.nn.sigmoid(scale * total_of(sums)) - labels[...]
    errs[...] = spread(errors, samples)
    acc[...] = jnp.zeros_like(acc)
    dense[...] = jnp.zeros_like(dense)
    tops[...] = jnp.zeros_like(tops)
    lanes = iota((samples, 128), 1)

    def step(j, carry):
        live = tab[LIVE, j].astype(f32)
        slot, first = tab[SLOT, j], tab[FIRST, j]
        va, vb = ft[first], second[j]
        gradient = dot_lhs(split(va.astype(f32) * errs[...]), vb, ATB)
        updated = mats[slot] - (rate * live) * gradient
        moved[j] = updated
        pair = split(updated * live)
        mixed = dot_rhs(va, pair, AB)
        acc[...] += mixed * vb.astype(f32)
        stash[j] = mixed
        tops[...] = jnp.where(lanes == j, peaks(mixed), tops[...])
        toward = dot_rhs(vb, pair, ABT)
        at = pl.ds(pl.multiple_of(first * rows, 8), rows)
        for i in range(n_x):
            dense[i, at] += toward[i * rows : (i + 1) * rows]
        return carry

    lax.fori_loop(0, second.shape[0], step, 0, unroll=2)

    k = exponent(tops[...])
    up = LEVELS * scale_of(-k)
    common = digits(row_sums(acc[...] * (1.0 / 128.0)))
    for i in range(n_x):
        part = slice(i * rows, (i + 1) * rows)
        lying = jnp.transpose(tile_of(128, [k[part]]))
        for j in range(second.shape[0]):
            d = j * n_x + i
            out[d, 0:rows] = whole(stash[j, part] * up[part, j : j + 1])
            out[d, rows : rows + 8] = whole(tile_of(8, [lying[j : j + 1]] + common))

    x = tab[MY_X, 0]
    own[...] = dense[x]
    lanes = iota((128, 128), 1)
    far = [lax.rem(x + r, n_x) for r in range(1, n_x)]
    high = jnp.zeros((128, 128), f32)
    for i, to in enumerate(far):
        for t in range(parts):
            top = peaks(dense[to, t * 128 : (t + 1) * 128])
            high = jnp.where(lanes == i * parts + t, top, high)
    k = exponent(high)
    up = LEVELS * scale_of(-k)
    lying = jnp.transpose(k)
    for i, (to, ref) in enumerate(zip(far, (to_1, to_2, to_3))):
        for t in range(parts):
            lane = i * parts + t
            part = dense[to, t * 128 : (t + 1) * 128]
            ref[t * 128 : (t + 1) * 128] = whole(part * up[:, lane : lane + 1])
        mine = lying[i * parts : (i + 1) * parts]
        ref[size : size + 8] = whole(tile_of(8, [mine]))


def across_kernel(served, got, own, from_1, from_2, from_3, out, sums, parted):
    n_x, n_z = served.shape[0], out.shape[0]
    wide = out.shape[1] - 16
    few = wide // 16
    size, rows = own.shape[0], n_z * few
    parts = size // 128

    sides = (from_1, from_2, from_3)
    exps = [real(ref[size : size + 8])[0:parts] for ref in sides]
    down = jnp.transpose(tile_of(128, exps))
    down = scale_of(down) * (1.0 / LEVELS)
    for t in range(parts):
        part = slice(t * 128, (t + 1) * 128)
        total = own[part]
        for i, ref in enumerate(sides):
            lane = i * parts + t
            total = total + real(ref[part]) * down[:, lane : lane + 1]
        sums[part] = total

    tiles = [real(got[d, rows : rows + 8]) for d in range(got.shape[0])]
    down = scale_of(upright([t[0:1] for t in tiles], rows)) * (1.0 / LEVELS)
    for d in range(got.shape[0]):
        field = served[d % n_x, SPARE + d // n_x]
        at = pl.ds(pl.multiple_of(field * rows, 8), rows)
        sums[at] += real(got[d, 0:rows]) * down[:, d : d + 1]

    for f in range(16):
        for z in range(n_z):
            start = f * rows + z * few
            parted[z, f * few : (f + 1) * few] = sums[start : start + few]
    lanes = iota((wide, 128), 1)
    tops = jnp.zeros((wide, 128), f32)
    for z in range(n_z):
        tops = jnp.where(lanes == z, peaks(parted[z]), tops)
    k = exponent(tops)
    up = LEVELS * scale_of(-k)
    if wide < 128:
        k = tile_of(128, [k])
    lying = [jnp.transpose(k[n * 128 : (n + 1) * 128]) for n in range(k.shape[0] // 128)]
    common = digits(undigits(tiles, 1))
    for z in range(n_z):
        out[z, 0:wide] = whole(parted[z] * up[:, z : z + 1])
        mine = [part[z : z + 1] for part in lying]
        out[z, wide : wide + 16] = whole(tile_of(16, mine + common))


def last_kernel(
    scale, rate, tab, ft, second, moved, got, labels, logits, grads, mats, errs, sums
):
    samples = second.shape[1]
    few = grads.shape[0]
    wide = 16 * few
    tiles = [real(got[i, wide : wide + 16]) for i in range(got.shape[0])]
    high = -(-wide // 128)
    exps = [upright([t[n : n + 1] for t in tiles], min(wide, 128)) for n in range(high)]
    down = scale_of(jnp.concatenate(exps, axis=0)) * (1.0 / LEVELS)
    value = scale * undigits(tiles, high)
    logits[...] = value
    errs[...] = spread(jax.nn.sigmoid(value) - labels[...], samples)
    total = real(got[0, 0:wide]) * down[:, 0:1]
    for i in range(1, got.shape[0]):
        total = total + real(got[i, 0:wide]) * down[:, i : i + 1]
    sums[...] = total * (1.0 / math.sqrt(128.0))
    for b in range(few):
        mine = errs[pl.ds(tab[MY_OWN, 0] * few + b, 1)]
        grads[b] = sums[pl.ds(b, 16, stride=few)] * mine

    def step(j, carry):
        live = tab[LIVE, j].astype(f32)
        weighted = split(ft[tab[FIRST, j]].astype(f32) * errs[...])
        mats[tab[SLOT, j]] = moved[j] - (rate * live) * dot_lhs(weighted, second[j], ATB)
        return carry

    lax.fori_loop(0, second.shape[0], step, 0, unroll=4)


def call(kernel, outs, n_in, scratch=(), smem=True):
    specs = [pl.BlockSpec(memory_space=pltpu.VMEM)] * n_in
    if smem:
        specs[0] = pl.BlockSpec(memory_space=pltpu.SMEM)
    out_specs = [pl.BlockSpec(memory_space=pltpu.VMEM)] * len(outs)
    return pl.pallas_call(
        kernel,
        out_shape=outs,
        in_specs=specs,
        out_specs=out_specs,
        scratch_shapes=list(scratch),
        compiler_params=pltpu.CompilerParams(vmem_limit_bytes=16 << 20),
    )


def shape(dims, dtype=f32):
    return jax.ShapeDtypeStruct(dims, dtype)


def swap(x, axes):
    return lax.all_to_all(x, axes, split_axis=0, concat_axis=0, tiled=True)


def on_device(fields, labels, pair_first, pair_second, pair_count, pair_mats):
    groups, owners = lax.axis_size(GRP), lax.axis_size(OWN)
    n_x, n_z = lax.axis_size("x"), lax.axis_size("z")
    me = lax.axis_index(GRP)
    samples, per_block, feature = fields.shape
    slots = pair_first.shape[2]
    scale = logit_gain / math.sqrt(groups * owners * slots)
    rate = step_size * scale / (samples * feature)
    few = samples // owners

    table = pair_second[:, 0, :]
    blocks = table // per_block
    served = jnp.sum(jnp.where(blocks == me, table - me * per_block, 0), axis=1)
    mine = lax.dynamic_index_in_dim(blocks, me, 0, keepdims=False)
    picked = mine[:, None] == jnp.arange(slots, dtype=jnp.int32)[None, :]
    slot_ids = jnp.arange(slots, dtype=jnp.int32)[:, None]
    slot_of = jnp.sum(jnp.where(picked, slot_ids, 0), axis=0)
    first_of = jnp.sum(jnp.where(picked, (pair_first[0, 0] - me * per_block)[:, None], 0), axis=0)
    live = (slot_of < pair_count[0, 0]).astype(jnp.int32)
    places = [lax.axis_index(OWN), me, lax.axis_index("x")]
    places = [jnp.full((slots,), place, jnp.int32) for place in places]
    tab = jnp.stack([slot_of, first_of, live, served] + places)

    ft = jnp.transpose(fields, (1, 0, 2))
    mats = pair_mats[0, 0]
    targets = jnp.pad(labels.astype(f32), (0, 256 - samples)).reshape(2, 128)

    sent = call(gather_kernel, [shape((slots, samples, feature), bf16)], 2)(tab, ft)[0]
    second = swap(sent, GRP)
    acc = pltpu.VMEM((samples, 128), f32)
    part = call(partial_kernel, [shape((groups * n_x, 2, 128))], 4, [acc])(tab, ft, second, mats)[0]
    out = [shape((n_z, 2, 128)), shape((n_x, 128), jnp.int32)]
    part, near = call(sum_kernel, out, 2)(tab, swap(part, GRP + ("x",)))
    sums = swap(part, "z")

    rows, wide = samples // n_x, per_block * few
    size = per_block * rows
    side = shape((size + 8, feature), jnp.int16)
    moved, out, own, *sides = call(
        functools.partial(terms_kernel, scale, rate),
        [
            shape(mats.shape),
            shape((groups * n_x, rows + 8, feature), jnp.int16),
            shape((size, feature)),
            side,
            side,
            side,
        ],
        6,
        [
            acc,
            acc,
            pltpu.VMEM((slots, samples, feature), f32),
            acc,
            pltpu.VMEM((n_x, size, feature), f32),
        ],
    )(tab, ft, second, mats, sums, targets)
    got = swap(out, GRP + ("x",))
    sides = [
        lax.ppermute(side, "x", [(i, (i + r) % n_x) for i in range(n_x)])
        for r, side in enumerate(sides, 1)
    ]
    out = [shape((n_z, wide + 16, feature), jnp.int16)]
    room = [pltpu.VMEM((size, feature), f32), pltpu.VMEM((n_z, wide, feature), f32)]
    got = call(across_kernel, out, 6, room)(near, got, own, *sides)[0]
    got = swap(got, "z")
    logits, grads, mats = call(
        functools.partial(last_kernel, scale, rate),
        [shape((2, 128)), shape((few, per_block, feature)), shape(mats.shape)],
        6,
        [acc, pltpu.VMEM((per_block * few, 128), f32)],
    )(tab, ft, second, moved, got, targets)
    return logits.reshape(256)[:samples], grads, mats[None, None]


def solution(mesh):
    n_grp, n_own = mesh.devices.shape
    sizes = (n_grp // 2, 2, 4, n_own // 4)
    split_mesh = Mesh(mesh.devices.reshape(sizes), ("y", "core", "x", "z"))
    in_specs = (
        P(None, GRP, None),
        P(),
        P(GRP, OWN, None),
        P(None, OWN, None),
        P(GRP, OWN),
        P(GRP, OWN, None, None, None),
    )
    out_specs = (P(), P(OWN, GRP, None), P(GRP, OWN, None, None, None))
    return jax.shard_map(
        on_device, mesh=split_mesh, in_specs=in_specs, out_specs=out_specs, check_vma=False
    )
```

```python
import functools
import math

import jax
import jax.numpy as jnp
from jax import lax
from jax.experimental import pallas as pl
from jax.experimental.pallas import tpu as pltpu
from jax.sharding import Mesh
from jax.sharding import PartitionSpec as P

GRP = ("y", "core")
OWN = ("x", "z")
logit_gain = 1.5
step_size = 1000.0
f32 = jnp.float32
bf16 = jnp.bfloat16

SLOT, FIRST, LIVE, SERVED, MY_OWN, MY_GRP, MY_X = range(7)
SPARE = 64


def split(x):
    hi = x.astype(bf16)
    return hi, (x - hi.astype(f32)).astype(bf16)


def dot(a, b, dims):
    return lax.dot_general(a, b, (dims, ((), ())), preferred_element_type=f32)


def dot_rhs(a, pair, dims):
    return dot(a, pair[0], dims) + dot(a, pair[1], dims)


def dot_lhs(pair, b, dims):
    return dot(pair[0], b, dims) + dot(pair[1], b, dims)


AB, ABT, ATB = ((1,), (0,)), ((1,), (1,)), ((0,), (0,))


def row_sums(acc):
    ones = jnp.ones((8, 128), f32)
    exact = functools.partial(
        lax.dot_general,
        dimension_numbers=(ABT, ((), ())),
        precision=lax.Precision.HIGHEST,
        preferred_element_type=f32,
    )
    low = exact(ones, acc[:128])
    rest = acc[128:]
    high = exact(ones, jnp.concatenate([rest, jnp.zeros((256 - acc.shape[0], 128), f32)], axis=0))
    return jnp.concatenate([low[0:1], high[0:1]], axis=0)


def spread(chunk, samples):
    low = jnp.transpose(jnp.broadcast_to(chunk[0:1], (128, 128)))
    high = jnp.transpose(jnp.broadcast_to(chunk[1:2], (128, 128)))
    return jnp.concatenate([low, high[: samples - 128]], axis=0)


def gather_kernel(tab, ft, out):
    @pl.loop(0, out.shape[0])
    def _(j):
        out[j] = ft[tab[SERVED, j]]


def partial_kernel(tab, ft, second, mats, out, acc):
    acc[...] = jnp.zeros_like(acc)

    def step(j, carry):
        live = tab[LIVE, j].astype(f32)
        mixed = dot_rhs(ft[tab[FIRST, j]], split(mats[tab[SLOT, j]] * live), AB)
        acc[...] += mixed * second[j].astype(f32)
        return carry

    lax.fori_loop(0, second.shape[0], step, 0, unroll=4)
    chunk = row_sums(acc[...] * (1.0 / 128.0))
    lanes = iota((2, 128), 1) + 128 * (1 - iota((2, 128), 0))
    for j in range(second.shape[0]):
        chunk = jnp.where(lanes == SPARE + j, tab[SERVED, j].astype(f32), chunk)
    for i in range(out.shape[0]):
        out[i] = chunk


def sum_kernel(tab, parts, out, served):
    total = total_of(parts)
    for i in range(out.shape[0]):
        out[i] = total
    n_x = served.shape[0]
    near = parts[pl.ds(tab[MY_GRP, 0] * n_x, n_x)]
    lanes = iota((1, 128), 1)
    mine = (lanes >= SPARE) & (lanes < SPARE + 16)
    for i in range(n_x):
        served[i : i + 1] = jnp.where(mine, near[i, 1:2], 0.0).astype(jnp.int32)


def total_of(parts):
    total = parts[0]
    for i in range(1, parts.shape[0]):
        total = total + parts[i]
    return total


LEVELS = 32000.0
OCTAVE = 64.0


def exponent(peak):
    return jnp.ceil(OCTAVE * jnp.log2(jnp.maximum(peak, 1e-30)))


def scale_of(k):
    return jnp.exp2(k * (1.0 / OCTAVE))


def whole(x):
    return jnp.round(x).astype(jnp.int32).astype(jnp.int16)


def real(x):
    return x.astype(jnp.int32).astype(f32)


def peaks(x):
    return jnp.max(jnp.abs(x), axis=1, keepdims=True)


def iota(dims, axis):
    return lax.broadcasted_iota(jnp.int32, dims, axis)


def tile_of(height, pieces):
    used = sum(p.shape[0] for p in pieces)
    return jnp.concatenate(pieces + [jnp.zeros((height - used, 128), f32)], axis=0)


def digits(pair):
    k = exponent(jnp.max(peaks(pair), axis=0, keepdims=True))
    wide = pair * (LEVELS * scale_of(-k))
    high = jnp.round(wide)
    return [high, (wide - high) * LEVELS, jnp.broadcast_to(k, (1, 128))]


def undigit(tile, at):
    s = scale_of(tile[at + 4 : at + 5]) * (1.0 / LEVELS)
    return s * (tile[at : at + 2] + tile[at + 2 : at + 4] * (1.0 / LEVELS))


def undigits(tiles, at):
    total = undigit(tiles[0], at)
    for t in tiles[1:]:
        total = total + undigit(t, at)
    return total


def upright(rows, height):
    tall = jnp.concatenate(rows + [jnp.zeros((128 - len(rows), 128), f32)], axis=0)
    return jnp.transpose(tall)[:height]


def terms_kernel(
    scale, rate, tab, ft, second, mats, sums, labels,
    out_hbm, own_hbm, to_1, to_2, to_3, acc, errs, stash, tops, dense, out, to_all, sems,
):
    samples = second.shape[1]
    n_x, size = dense.shape[0], dense.shape[1]
    rows, parts = samples // n_x, size // 128
    errors = jax.nn.sigmoid(scale * total_of(sums)) - labels[...]
    errs[...] = spread(errors, samples)
    acc[...] = jnp.zeros_like(acc)
    dense[...] = jnp.zeros_like(dense)
    tops[...] = jnp.zeros_like(tops)
    lanes = iota((samples, 128), 1)

    def step(j, carry):
        live = tab[LIVE, j].astype(f32)
        slot, first = tab[SLOT, j], tab[FIRST, j]
        va, vb = ft[first], second[j]
        gradient = dot_lhs(split(va.astype(f32) * errs[...]), vb, ATB)
        updated = mats[slot] - (rate * live) * gradient
        pair = split(updated * live)
        mixed = dot_rhs(va, pair, AB)
        acc[...] += mixed * vb.astype(f32)
        stash[j] = mixed
        tops[...] = jnp.where(lanes == j, peaks(mixed), tops[...])
        toward = dot_rhs(vb, pair, ABT)
        at = pl.ds(pl.multiple_of(first * rows, 8), rows)
        for i in range(n_x):
            dense[i, at] += toward[i * rows : (i + 1) * rows]
        return carry

    lax.fori_loop(0, second.shape[0], step, 0, unroll=2)

    x = tab[MY_X, 0]
    copies = [pltpu.make_async_copy(dense.at[x], own_hbm, sems.at[0])]
    copies[0].start()
    lanes = iota((128, 128), 1)
    far = [lax.rem(x + r, n_x) for r in range(1, n_x)]
    high = jnp.zeros((128, 128), f32)
    for i, to in enumerate(far):
        for t in range(parts):
            top = peaks(dense[to, t * 128 : (t + 1) * 128])
            high = jnp.where(lanes == i * parts + t, top, high)
    k = exponent(high)
    up = LEVELS * scale_of(-k)
    lying = jnp.transpose(k)
    for i, (to, ref) in enumerate(zip(far, (to_1, to_2, to_3))):
        for t in range(parts):
            lane = i * parts + t
            part = dense[to, t * 128 : (t + 1) * 128]
            to_all[i, t * 128 : (t + 1) * 128] = whole(part * up[:, lane : lane + 1])
        mine = lying[i * parts : (i + 1) * parts]
        to_all[i, size : size + 8] = whole(tile_of(8, [mine]))
        copies.append(pltpu.make_async_copy(to_all.at[i], ref, sems.at[1 + i]))
        copies[-1].start()

    k = exponent(tops[...])
    up = LEVELS * scale_of(-k)
    zero = jnp.zeros((1, 128), f32)
    tail = tile_of(8, [zero] + digits(row_sums(acc[...] * (1.0 / 128.0))))
    top_row = iota((8, 128), 0) == 0
    for i in range(n_x):
        part = slice(i * rows, (i + 1) * rows)
        lying = jnp.transpose(tile_of(128, [k[part]]))
        for j in range(second.shape[0]):
            d = j * n_x + i
            out[d, 0:rows] = whole(stash[j, part] * up[part, j : j + 1])
            out[d, rows : rows + 8] = whole(jnp.where(top_row, lying[j : j + 1], tail))

    copies.append(pltpu.make_async_copy(out, out_hbm, sems.at[n_x]))
    copies[-1].start()
    for copy in copies:
        copy.wait()


def across_kernel(
    served, got_hbm, own_hbm, from_1, from_2, from_3, out, sums, parted, got, own, from_all, sems
):
    copies = [pltpu.make_async_copy(own_hbm, own, sems.at[0])]
    for i, ref in enumerate((from_1, from_2, from_3)):
        copies.append(pltpu.make_async_copy(ref, from_all.at[i], sems.at[1 + i]))
    last = pltpu.make_async_copy(got_hbm, got, sems.at[4])
    for copy in copies + [last]:
        copy.start()
    for copy in copies:
        copy.wait()
    n_x, n_z = served.shape[0], out.shape[0]
    wide = out.shape[1] - 16
    few = wide // 16
    size, rows = own.shape[0], n_z * few
    parts = size // 128

    sides = range(from_all.shape[0])
    exps = [real(from_all[i, size : size + 8])[0:parts] for i in sides]
    down = jnp.transpose(tile_of(128, exps))
    down = scale_of(down) * (1.0 / LEVELS)
    for t in range(parts):
        part = slice(t * 128, (t + 1) * 128)
        total = own[part]
        for i in sides:
            lane = i * parts + t
            total = total + real(from_all[i, part]) * down[:, lane : lane + 1]
        sums[part] = total

    last.wait()
    tiles = [real(got[d, rows : rows + 8]) for d in range(got.shape[0])]
    down = scale_of(upright([t[0:1] for t in tiles], rows)) * (1.0 / LEVELS)
    for d in range(got.shape[0]):
        field = served[d % n_x, SPARE + d // n_x]
        at = pl.ds(pl.multiple_of(field * rows, 8), rows)
        sums[at] += real(got[d, 0:rows]) * down[:, d : d + 1]

    for f in range(16):
        for z in range(n_z):
            start = f * rows + z * few
            parted[z, f * few : (f + 1) * few] = sums[start : start + few]
    lanes = iota((wide, 128), 1)
    tops = jnp.zeros((wide, 128), f32)
    for z in range(n_z):
        tops = jnp.where(lanes == z, peaks(parted[z]), tops)
    k = exponent(tops)
    up = LEVELS * scale_of(-k)
    if wide < 128:
        k = tile_of(128, [k])
    lying = [jnp.transpose(k[n * 128 : (n + 1) * 128]) for n in range(k.shape[0] // 128)]
    common = digits(undigits(tiles, 1))
    for z in range(n_z):
        out[z, 0:wide] = whole(parted[z] * up[:, z : z + 1])
        mine = [part[z : z + 1] for part in lying]
        out[z, wide : wide + 16] = whole(tile_of(16, mine + common))


def last_kernel(
    scale, rate, tab, ft, second, mats_in, got, first_sums, labels, logits, grads, mats, errs, sums
):
    samples = second.shape[1]
    few = grads.shape[0]
    wide = 16 * few
    tiles = [real(got[i, wide : wide + 16]) for i in range(got.shape[0])]
    high = -(-wide // 128)
    exps = [upright([t[n : n + 1] for t in tiles], min(wide, 128)) for n in range(high)]
    down = scale_of(jnp.concatenate(exps, axis=0)) * (1.0 / LEVELS)
    value = scale * undigits(tiles, high)
    logits[...] = value
    errors = jax.nn.sigmoid(value) - labels[...]
    errs[...] = spread(errors, samples)
    total = real(got[0, 0:wide]) * down[:, 0:1]
    for i in range(1, got.shape[0]):
        total = total + real(got[i, 0:wide]) * down[:, i : i + 1]
    sums[...] = total * (1.0 / math.sqrt(128.0))
    for b in range(few):
        mine = errs[pl.ds(tab[MY_OWN, 0] * few + b, 1)]
        grads[b] = sums[pl.ds(b, 16, stride=few)] * mine
    earlier = jax.nn.sigmoid(scale * total_of(first_sums)) - labels[...]
    errs[...] = spread(errors + earlier, samples)

    def step(j, carry):
        live = tab[LIVE, j].astype(f32)
        weighted = split(ft[tab[FIRST, j]].astype(f32) * errs[...])
        slot = tab[SLOT, j]
        mats[slot] = mats_in[slot] - (rate * live) * dot_lhs(weighted, second[j], ATB)
        return carry

    lax.fori_loop(0, second.shape[0], step, 0, unroll=4)


def call(kernel, outs, n_in, scratch=(), smem=True, far_in=(), far_out=False, room=16):
    specs = [pl.BlockSpec(memory_space=pltpu.VMEM)] * n_in
    if smem:
        specs[0] = pl.BlockSpec(memory_space=pltpu.SMEM)
    for i in far_in:
        specs[i] = pl.BlockSpec(memory_space=pltpu.HBM)
    space = pltpu.HBM if far_out else pltpu.VMEM
    return pl.pallas_call(
        kernel,
        out_shape=outs,
        in_specs=specs,
        out_specs=[pl.BlockSpec(memory_space=space)] * len(outs),
        scratch_shapes=list(scratch),
        compiler_params=pltpu.CompilerParams(vmem_limit_bytes=room << 20),
    )


def shape(dims, dtype=f32):
    return jax.ShapeDtypeStruct(dims, dtype)


def swap(x, axes):
    return lax.all_to_all(x, axes, split_axis=0, concat_axis=0, tiled=True)


def on_device(fields, labels, pair_first, pair_second, pair_count, pair_mats):
    groups, owners = lax.axis_size(GRP), lax.axis_size(OWN)
    n_x, n_z = lax.axis_size("x"), lax.axis_size("z")
    me = lax.axis_index(GRP)
    samples, per_block, feature = fields.shape
    slots = pair_first.shape[2]
    scale = logit_gain / math.sqrt(groups * owners * slots)
    rate = step_size * scale / (samples * feature)
    few = samples // owners

    table = pair_second[:, 0, :]
    blocks = table // per_block
    served = jnp.sum(jnp.where(blocks == me, table - me * per_block, 0), axis=1)
    mine = lax.dynamic_index_in_dim(blocks, me, 0, keepdims=False)
    picked = mine[:, None] == jnp.arange(slots, dtype=jnp.int32)[None, :]
    slot_ids = jnp.arange(slots, dtype=jnp.int32)[:, None]
    slot_of = jnp.sum(jnp.where(picked, slot_ids, 0), axis=0)
    first_of = jnp.sum(jnp.where(picked, (pair_first[0, 0] - me * per_block)[:, None], 0), axis=0)
    live = (slot_of < pair_count[0, 0]).astype(jnp.int32)
    places = [lax.axis_index(OWN), me, lax.axis_index("x")]
    places = [jnp.full((slots,), place, jnp.int32) for place in places]
    tab = jnp.stack([slot_of, first_of, live, served] + places)

    ft = jnp.transpose(fields, (1, 0, 2))
    mats = pair_mats[0, 0]
    targets = jnp.pad(labels.astype(f32), (0, 256 - samples)).reshape(2, 128)

    sent = call(gather_kernel, [shape((slots, samples, feature), bf16)], 2)(tab, ft)[0]
    second = swap(sent, GRP)
    acc = pltpu.VMEM((samples, 128), f32)
    part = call(partial_kernel, [shape((groups * n_x, 2, 128))], 4, [acc])(tab, ft, second, mats)[0]
    out = [shape((n_z, 2, 128)), shape((n_x, 128), jnp.int32)]
    part, near = call(sum_kernel, out, 2)(tab, swap(part, GRP + ("x",)))
    sums = swap(part, "z")

    rows, wide = samples // n_x, per_block * few
    size = per_block * rows
    side = shape((size + 8, feature), jnp.int16)
    out, own, *sides = call(
        functools.partial(terms_kernel, scale, rate),
        [
            shape((groups * n_x, rows + 8, feature), jnp.int16),
            shape((size, feature)),
            side,
            side,
            side,
        ],
        6,
        [
            acc,
            acc,
            pltpu.VMEM((slots, samples, feature), f32),
            acc,
            pltpu.VMEM((n_x, size, feature), f32),
            pltpu.VMEM((groups * n_x, rows + 8, feature), jnp.int16),
            pltpu.VMEM((n_x - 1, size + 8, feature), jnp.int16),
            pltpu.SemaphoreType.DMA((n_x + 1,)),
        ],
        far_out=True,
        room=60,
    )(tab, ft, second, mats, sums, targets)
    got = swap(out, GRP + ("x",))
    sides = [
        lax.ppermute(side, "x", [(i, (i + r) % n_x) for i in range(n_x)])
        for r, side in enumerate(sides, 1)
    ]
    out = [shape((n_z, wide + 16, feature), jnp.int16)]
    room = [
        pltpu.VMEM((size, feature), f32),
        pltpu.VMEM((n_z, wide, feature), f32),
        pltpu.VMEM((groups * n_x, rows + 8, feature), jnp.int16),
        pltpu.VMEM((size, feature), f32),
        pltpu.VMEM((n_x - 1, size + 8, feature), jnp.int16),
        pltpu.SemaphoreType.DMA((n_x + 1,)),
    ]
    got = call(across_kernel, out, 6, room, far_in=range(1, 6), room=16)(near, got, own, *sides)[0]
    got = swap(got, "z")
    logits, grads, mats = call(
        functools.partial(last_kernel, scale, rate),
        [shape((2, 128)), shape((few, per_block, feature)), shape(mats.shape)],
        7,
        [acc, pltpu.VMEM((per_block * few, 128), f32)],
    )(tab, ft, second, mats, got, sums, targets)
    return logits.reshape(256)[:samples], grads, mats[None, None]


def solution(mesh):
    n_grp, n_own = mesh.devices.shape
    sizes = (n_grp // 2, 2, 4, n_own // 4)
    split_mesh = Mesh(mesh.devices.reshape(sizes), ("y", "core", "x", "z"))
    in_specs = (
        P(None, GRP, None),
        P(),
        P(GRP, OWN, None),
        P(None, OWN, None),
        P(GRP, OWN),
        P(GRP, OWN, None, None, None),
    )
    out_specs = (P(), P(OWN, GRP, None), P(GRP, OWN, None, None, None))
    return jax.shard_map(
        on_device, mesh=split_mesh, in_specs=in_specs, out_specs=out_specs, check_vma=False
    )
```

```python
import functools
import math

import jax
import jax.numpy as jnp
from jax import lax
from jax.experimental import pallas as pl
from jax.experimental.pallas import tpu as pltpu
from jax.sharding import Mesh
from jax.sharding import PartitionSpec as P

GRP = ("y", "core")
OWN = ("x", "z")
logit_gain = 1.5
step_size = 1000.0
f32 = jnp.float32
bf16 = jnp.bfloat16

SLOT, FIRST, LIVE, SERVED, MY_OWN, MY_X = range(6)

PARTIAL_GROUP, TERMS_GROUP, LAST_GROUP = 16, 8, 16
SPARE = 64


def split(x):
    hi = x.astype(bf16)
    return hi, (x - hi.astype(f32)).astype(bf16)


def dot(a, b, dims):
    return lax.dot_general(a, b, (dims, ((), ())), preferred_element_type=f32)


def beside(x):
    return jnp.concatenate(split(x), axis=1)


def twice(x):
    return jnp.concatenate([x, x], axis=1)


AB, ABT, ATB = ((1,), (0,)), ((1,), (1,)), ((0,), (0,))


def row_sums(acc):
    ones = jnp.ones((8, 128), f32)
    exact = functools.partial(
        lax.dot_general,
        dimension_numbers=(ABT, ((), ())),
        precision=lax.Precision.HIGHEST,
        preferred_element_type=f32,
    )
    low = exact(ones, acc[:128])
    rest = acc[128:]
    high = exact(ones, jnp.concatenate([rest, jnp.zeros((256 - acc.shape[0], 128), f32)], axis=0))
    return jnp.concatenate([low[0:1], high[0:1]], axis=0)


def spread(chunk, samples):
    low = jnp.transpose(jnp.broadcast_to(chunk[0:1], (128, 128)))
    high = jnp.transpose(jnp.broadcast_to(chunk[1:2], (128, 128)))
    return jnp.concatenate([low, high[: samples - 128]], axis=0)


def gather_kernel(tab, ft, out):
    @pl.loop(0, out.shape[0])
    def _(j):
        out[j] = ft[tab[SERVED, j]]


def partial_kernel(tab, ft, second, mats, out, acc):
    acc[...] = jnp.zeros_like(acc)

    group = math.gcd(PARTIAL_GROUP, second.shape[0])

    def step(q, carry):
        js = [q * group + i for i in range(group)]
        pairs = [split(mats[tab[SLOT, j]] * tab[LIVE, j].astype(f32)) for j in js]
        mixed = [
            dot(twice(ft[tab[FIRST, j]]), jnp.concatenate(pair, axis=0), AB)
            for j, pair in zip(js, pairs)
        ]
        total = acc[...]
        for j, m in zip(js, mixed):
            total = total + m * second[j].astype(f32)
        acc[...] = total
        return carry

    lax.fori_loop(0, second.shape[0] // group, step, 0)
    chunk = row_sums(acc[...] * (1.0 / 128.0))
    lanes = iota((2, 128), 1) + 128 * (1 - iota((2, 128), 0))
    for j in range(second.shape[0]):
        chunk = jnp.where(lanes == SPARE + j, tab[SERVED, j].astype(f32), chunk)
    for i in range(out.shape[0]):
        out[i] = chunk


def sum_kernel(parts, out, served):
    total = total_of(parts)
    for i in range(out.shape[0]):
        out[i] = total
    n_x = served.shape[0]
    near = parts[pl.ds(lax.axis_index(GRP) * n_x, n_x)]
    lanes = iota((1, 128), 1)
    mine = (lanes >= SPARE) & (lanes < SPARE + 16)
    for i in range(n_x):
        served[i : i + 1] = jnp.where(mine, near[i, 1:2], 0.0).astype(jnp.int32)


def total_of(parts):
    total = parts[0]
    for i in range(1, parts.shape[0]):
        total = total + parts[i]
    return total


LEVELS = 32000.0
OCTAVE = 64.0


def exponent(peak):
    return jnp.ceil(OCTAVE * jnp.log2(jnp.maximum(peak, 1e-30)))


def scale_of(k):
    return jnp.exp2(k * (1.0 / OCTAVE))


def whole(x):
    return jnp.round(x).astype(jnp.int32).astype(jnp.int16)


def real(x):
    return x.astype(jnp.int32).astype(f32)


def peaks(x):
    return jnp.max(jnp.abs(x), axis=1, keepdims=True)


def iota(dims, axis):
    return lax.broadcasted_iota(jnp.int32, dims, axis)


def tile_of(height, pieces):
    used = sum(p.shape[0] for p in pieces)
    return jnp.concatenate(pieces + [jnp.zeros((height - used, 128), f32)], axis=0)


def digits(pair):
    k = exponent(jnp.max(peaks(pair), axis=0, keepdims=True))
    wide = pair * (LEVELS * scale_of(-k))
    high = jnp.round(wide)
    return [high, (wide - high) * LEVELS, jnp.broadcast_to(k, (1, 128))]


def undigit(tile, at):
    s = scale_of(tile[at + 4 : at + 5]) * (1.0 / LEVELS)
    return s * (tile[at : at + 2] + tile[at + 2 : at + 4] * (1.0 / LEVELS))


def undigits(tiles, at):
    total = undigit(tiles[0], at)
    for t in tiles[1:]:
        total = total + undigit(t, at)
    return total


def upright(rows, height):
    tall = jnp.concatenate(rows + [jnp.zeros((128 - len(rows), 128), f32)], axis=0)
    return jnp.transpose(tall)[:height]


def terms_kernel(
    scale, rate, tab, ft, second, mats, sums, labels,
    out_hbm, own_hbm, to_1, to_2, to_3, acc, errs, stash, tops, dense, out, to_all, sems,
):
    samples = second.shape[1]
    n_x, size = dense.shape[0], dense.shape[1]
    rows, parts = samples // n_x, size // 128
    errors = jax.nn.sigmoid(scale * total_of(sums)) - labels[...]
    errs[...] = spread(errors, samples)
    acc[...] = jnp.zeros_like(acc)
    dense[...] = jnp.zeros_like(dense)
    tops[...] = jnp.zeros_like(tops)
    lanes = iota((samples, 128), 1)

    group = math.gcd(TERMS_GROUP, second.shape[0])

    def step(q, carry):
        js = [q * group + i for i in range(group)]
        lives = [tab[LIVE, j].astype(f32) for j in js]
        slots = [tab[SLOT, j] for j in js]
        firsts = [tab[FIRST, j] for j in js]
        vas, vbs = [ft[first] for first in firsts], [second[j] for j in js]
        e = errs[...]
        both = [dot(va, beside(vb.astype(f32) * e), ATB) for va, vb in zip(vas, vbs)]
        updated = [
            (mats[slot] - (rate * live) * (g[:, :128] + g[:, 128:])) * live
            for slot, live, g in zip(slots, lives, both)
        ]
        pairs = [split(m) for m in updated]
        mixed = [
            dot(twice(va), jnp.concatenate(pair, axis=0), AB) for va, pair in zip(vas, pairs)
        ]
        toward = [
            dot(twice(vb), jnp.concatenate(pair, axis=1), ABT) for vb, pair in zip(vbs, pairs)
        ]
        total, top = acc[...], tops[...]
        for j, m, vb in zip(js, mixed, vbs):
            stash[j] = m
            total = total + m * vb.astype(f32)
            top = jnp.where(lanes == j, peaks(m), top)
        acc[...] = total
        tops[...] = top
        for first, t in zip(firsts, toward):
            at = pl.ds(pl.multiple_of(first * rows, 8), rows)
            for i in range(n_x):
                dense[i, at] += t[i * rows : (i + 1) * rows]
        return carry

    lax.fori_loop(0, second.shape[0] // group, step, 0)

    x = tab[MY_X, 0]
    copies = [pltpu.make_async_copy(dense.at[x], own_hbm, sems.at[0])]
    copies[0].start()
    lanes = iota((128, 128), 1)
    far = [lax.rem(x + r, n_x) for r in range(1, n_x)]
    high = jnp.zeros((128, 128), f32)
    for i, to in enumerate(far):
        for t in range(parts):
            top = peaks(dense[to, t * 128 : (t + 1) * 128])
            high = jnp.where(lanes == i * parts + t, top, high)
    k = exponent(high)
    up = LEVELS * scale_of(-k)
    lying = jnp.transpose(k)
    for i, (to, ref) in enumerate(zip(far, (to_1, to_2, to_3))):
        for t in range(parts):
            lane = i * parts + t
            part = dense[to, t * 128 : (t + 1) * 128]
            to_all[i, t * 128 : (t + 1) * 128] = whole(part * up[:, lane : lane + 1])
        mine = lying[i * parts : (i + 1) * parts]
        to_all[i, size : size + 8] = whole(tile_of(8, [mine]))
        copies.append(pltpu.make_async_copy(to_all.at[i], ref, sems.at[1 + i]))
        copies[-1].start()

    k = exponent(tops[...])
    up = LEVELS * scale_of(-k)
    zero = jnp.zeros((1, 128), f32)
    tail = tile_of(8, [zero] + digits(row_sums(acc[...] * (1.0 / 128.0))))
    top_row = iota((8, 128), 0) == 0
    for i in range(n_x):
        part = slice(i * rows, (i + 1) * rows)
        lying = jnp.transpose(tile_of(128, [k[part]]))
        for j in range(second.shape[0]):
            d = j * n_x + i
            out[d, 0:rows] = whole(stash[j, part] * up[part, j : j + 1])
            out[d, rows : rows + 8] = whole(jnp.where(top_row, lying[j : j + 1], tail))

    copies.append(pltpu.make_async_copy(out, out_hbm, sems.at[n_x]))
    copies[-1].start()
    for copy in copies:
        copy.wait()


def across_kernel(
    served, got_hbm, own_hbm, from_1, from_2, from_3, out, sums, parted, got, own, from_all, sems
):
    copies = [pltpu.make_async_copy(own_hbm, own, sems.at[0])]
    for i, ref in enumerate((from_1, from_2, from_3)):
        copies.append(pltpu.make_async_copy(ref, from_all.at[i], sems.at[1 + i]))
    last = pltpu.make_async_copy(got_hbm, got, sems.at[4])
    for copy in copies + [last]:
        copy.start()
    for copy in copies:
        copy.wait()
    n_x, n_z = served.shape[0], out.shape[0]
    wide = out.shape[1] - 16
    few = wide // 16
    size, rows = own.shape[0], n_z * few
    parts = size // 128

    sides = range(from_all.shape[0])
    exps = [real(from_all[i, size : size + 8])[0:parts] for i in sides]
    down = jnp.transpose(tile_of(128, exps))
    down = scale_of(down) * (1.0 / LEVELS)
    for t in range(parts):
        part = slice(t * 128, (t + 1) * 128)
        total = own[part]
        for i in sides:
            lane = i * parts + t
            total = total + real(from_all[i, part]) * down[:, lane : lane + 1]
        sums[part] = total

    last.wait()
    tiles = [real(got[d, rows : rows + 8]) for d in range(got.shape[0])]
    down = scale_of(upright([t[0:1] for t in tiles], rows)) * (1.0 / LEVELS)
    for q in range(0, got.shape[0], 8):
        values = [real(got[d, 0:rows]) * down[:, d : d + 1] for d in range(q, q + 8)]
        for d, value in zip(range(q, q + 8), values):
            field = served[d % n_x, SPARE + d // n_x]
            at = pl.ds(pl.multiple_of(field * rows, 8), rows)
            sums[at] += value
    for f in range(16):
        for z in range(n_z):
            start = f * rows + z * few
            parted[z, f * few : (f + 1) * few] = sums[start : start + few]
    lanes = iota((wide, 128), 1)
    tops = jnp.zeros((wide, 128), f32)
    for z in range(n_z):
        tops = jnp.where(lanes == z, peaks(parted[z]), tops)
    k = exponent(tops)
    up = LEVELS * scale_of(-k)
    if wide < 128:
        k = tile_of(128, [k])
    lying = [jnp.transpose(k[n * 128 : (n + 1) * 128]) for n in range(k.shape[0] // 128)]
    common = digits(undigits(tiles, 1))
    for z in range(n_z):
        out[z, 0:wide] = whole(parted[z] * up[:, z : z + 1])
        mine = [part[z : z + 1] for part in lying]
        out[z, wide : wide + 16] = whole(tile_of(16, mine + common))


def last_kernel(
    scale, rate, tab, ft, second, mats_in, got, first_sums, labels, logits, grads, mats, errs, sums
):
    samples = second.shape[1]
    few = grads.shape[0]
    wide = 16 * few
    tiles = [real(got[i, wide : wide + 16]) for i in range(got.shape[0])]
    high = -(-wide // 128)
    exps = [upright([t[n : n + 1] for t in tiles], min(wide, 128)) for n in range(high)]
    down = scale_of(jnp.concatenate(exps, axis=0)) * (1.0 / LEVELS)
    value = scale * undigits(tiles, high)
    logits[...] = value
    errors = jax.nn.sigmoid(value) - labels[...]
    errs[...] = spread(errors, samples)
    total = real(got[0, 0:wide]) * down[:, 0:1]
    for i in range(1, got.shape[0]):
        total = total + real(got[i, 0:wide]) * down[:, i : i + 1]
    sums[...] = total * (1.0 / math.sqrt(128.0))
    for b in range(few):
        mine = errs[pl.ds(tab[MY_OWN, 0] * few + b, 1)]
        grads[b] = sums[pl.ds(b, 16, stride=few)] * mine
    earlier = jax.nn.sigmoid(scale * total_of(first_sums)) - labels[...]
    errs[...] = spread(errors + earlier, samples)

    group = math.gcd(LAST_GROUP, second.shape[0])

    def step(q, carry):
        js = [q * group + i for i in range(group)]
        e = errs[...]
        both = [dot(ft[tab[FIRST, j]], beside(second[j].astype(f32) * e), ATB) for j in js]
        for j, g in zip(js, both):
            slot, live = tab[SLOT, j], tab[LIVE, j].astype(f32)
            mats[slot] = mats_in[slot] - (rate * live) * (g[:, :128] + g[:, 128:])
        return carry

    lax.fori_loop(0, second.shape[0] // group, step, 0)


def call(kernel, outs, n_in, scratch=(), smem=True, far_in=(), far_out=False, room=16):
    specs = [pl.BlockSpec(memory_space=pltpu.VMEM)] * n_in
    if smem:
        specs[0] = pl.BlockSpec(memory_space=pltpu.SMEM)
    for i in far_in:
        specs[i] = pl.BlockSpec(memory_space=pltpu.HBM)
    space = pltpu.HBM if far_out else pltpu.VMEM
    return pl.pallas_call(
        kernel,
        out_shape=outs,
        in_specs=specs,
        out_specs=[pl.BlockSpec(memory_space=space)] * len(outs),
        scratch_shapes=list(scratch),
        compiler_params=pltpu.CompilerParams(vmem_limit_bytes=room << 20),
    )


def shape(dims, dtype=f32):
    return jax.ShapeDtypeStruct(dims, dtype)


def swap(x, axes):
    return lax.all_to_all(x, axes, split_axis=0, concat_axis=0, tiled=True)


def on_device(fields, labels, pair_first, pair_second, pair_count, pair_mats):
    groups, owners = lax.axis_size(GRP), lax.axis_size(OWN)
    n_x, n_z = lax.axis_size("x"), lax.axis_size("z")
    me = lax.axis_index(GRP)
    samples, per_block, feature = fields.shape
    slots = pair_first.shape[2]
    scale = logit_gain / math.sqrt(groups * owners * slots)
    rate = step_size * scale / (samples * feature)
    few = samples // owners

    table = pair_second[:, 0, :]
    blocks = table // per_block
    served = jnp.sum(jnp.where(blocks == me, table - me * per_block, 0), axis=1)
    mine = lax.dynamic_index_in_dim(blocks, me, 0, keepdims=False)
    picked = mine[:, None] == jnp.arange(slots, dtype=jnp.int32)[None, :]
    slot_ids = jnp.arange(slots, dtype=jnp.int32)[:, None]
    slot_of = jnp.sum(jnp.where(picked, slot_ids, 0), axis=0)
    first_of = jnp.sum(jnp.where(picked, (pair_first[0, 0] - me * per_block)[:, None], 0), axis=0)
    live = (slot_of < pair_count[0, 0]).astype(jnp.int32)
    places = [lax.axis_index(OWN), lax.axis_index("x")]
    places = [jnp.full((slots,), place, jnp.int32) for place in places]
    tab = jnp.stack([slot_of, first_of, live, served] + places)

    ft = jnp.transpose(fields, (1, 0, 2))
    mats = pair_mats[0, 0]
    targets = jnp.pad(labels.astype(f32), (0, 256 - samples)).reshape(2, 128)

    sent = call(gather_kernel, [shape((slots, samples, feature), bf16)], 2)(tab, ft)[0]
    second = swap(sent, GRP)
    acc = pltpu.VMEM((samples, 128), f32)
    part = call(partial_kernel, [shape((groups * n_x, 2, 128))], 4, [acc])(tab, ft, second, mats)[0]
    out = [shape((n_z, 2, 128)), shape((n_x, 128), jnp.int32)]
    part, near = call(sum_kernel, out, 1, smem=False)(swap(part, GRP + ("x",)))
    sums = swap(part, "z")

    rows, wide = samples // n_x, per_block * few
    size = per_block * rows
    side = shape((size + 8, feature), jnp.int16)
    out, own, *sides = call(
        functools.partial(terms_kernel, scale, rate),
        [
            shape((groups * n_x, rows + 8, feature), jnp.int16),
            shape((size, feature)),
            side,
            side,
            side,
        ],
        6,
        [
            acc,
            acc,
            pltpu.VMEM((slots, samples, feature), f32),
            acc,
            pltpu.VMEM((n_x, size, feature), f32),
            pltpu.VMEM((groups * n_x, rows + 8, feature), jnp.int16),
            pltpu.VMEM((n_x - 1, size + 8, feature), jnp.int16),
            pltpu.SemaphoreType.DMA((n_x + 1,)),
        ],
        far_out=True,
        room=60,
    )(tab, ft, second, mats, sums, targets)
    got = swap(out, GRP + ("x",))
    sides = [
        lax.ppermute(side, "x", [(i, (i + r) % n_x) for i in range(n_x)])
        for r, side in enumerate(sides, 1)
    ]
    out = [shape((n_z, wide + 16, feature), jnp.int16)]
    room = [
        pltpu.VMEM((size, feature), f32),
        pltpu.VMEM((n_z, wide, feature), f32),
        pltpu.VMEM((groups * n_x, rows + 8, feature), jnp.int16),
        pltpu.VMEM((size, feature), f32),
        pltpu.VMEM((n_x - 1, size + 8, feature), jnp.int16),
        pltpu.SemaphoreType.DMA((n_x + 1,)),
    ]
    got = call(across_kernel, out, 6, room, far_in=range(1, 6), room=16)(near, got, own, *sides)[0]
    got = swap(got, "z")
    logits, grads, mats = call(
        functools.partial(last_kernel, scale, rate),
        [shape((2, 128)), shape((few, per_block, feature)), shape(mats.shape)],
        7,
        [acc, pltpu.VMEM((per_block * few, 128), f32)],
    )(tab, ft, second, mats, got, sums, targets)
    return logits.reshape(256)[:samples], grads, mats[None, None]


def solution(mesh):
    n_grp, n_own = mesh.devices.shape
    sizes = (n_grp // 2, 2, 4, n_own // 4)
    split_mesh = Mesh(mesh.devices.reshape(sizes), ("y", "core", "x", "z"))
    in_specs = (
        P(None, GRP, None),
        P(),
        P(GRP, OWN, None),
        P(None, OWN, None),
        P(GRP, OWN),
        P(GRP, OWN, None, None, None),
    )
    out_specs = (P(), P(OWN, GRP, None), P(GRP, OWN, None, None, None))
    return jax.shard_map(
        on_device, mesh=split_mesh, in_specs=in_specs, out_specs=out_specs, check_vma=False
    )
```

```python
import functools
import math

import jax
import jax.numpy as jnp
from jax import lax
from jax.experimental import pallas as pl
from jax.experimental.pallas import tpu as pltpu
from jax.sharding import Mesh
from jax.sharding import PartitionSpec as P

GRP = ("y", "core")
OWN = ("x", "z")
logit_gain = 1.5
step_size = 1000.0
f32 = jnp.float32
bf16 = jnp.bfloat16

SLOT, FIRST, LIVE, SERVED, MY_OWN, MY_X = range(6)

PARTIAL_GROUP, TERMS_GROUP, LAST_GROUP = 16, 8, 16
SPARE = 64


def split(x):
    hi = x.astype(bf16)
    return hi, (x - hi.astype(f32)).astype(bf16)


def dot(a, b, dims):
    return lax.dot_general(a, b, (dims, ((), ())), preferred_element_type=f32)


def beside(x):
    return jnp.concatenate(split(x), axis=1)


def twice(x):
    return jnp.concatenate([x, x], axis=1)


AB, ABT, ATB = ((1,), (0,)), ((1,), (1,)), ((0,), (0,))


def row_sums(acc):
    ones = jnp.ones((8, 128), f32)
    exact = functools.partial(
        lax.dot_general,
        dimension_numbers=(ABT, ((), ())),
        precision=lax.Precision.HIGHEST,
        preferred_element_type=f32,
    )
    low = exact(ones, acc[:128])
    rest = acc[128:]
    high = exact(ones, jnp.concatenate([rest, jnp.zeros((256 - acc.shape[0], 128), f32)], axis=0))
    return jnp.concatenate([low[0:1], high[0:1]], axis=0)


def spread(chunk, samples):
    low = jnp.transpose(jnp.broadcast_to(chunk[0:1], (128, 128)))
    high = jnp.transpose(jnp.broadcast_to(chunk[1:2], (128, 128)))
    return jnp.concatenate([low, high[: samples - 128]], axis=0)


def gather_kernel(tab, ft, out):
    @pl.loop(0, out.shape[0])
    def _(j):
        out[j] = ft[tab[SERVED, j]]


def partial_kernel(tab, ft, second, mats, out, acc):
    acc[...] = jnp.zeros_like(acc)

    group = math.gcd(PARTIAL_GROUP, second.shape[0])

    def step(q, carry):
        js = [q * group + i for i in range(group)]
        pairs = [split(mats[tab[SLOT, j]] * tab[LIVE, j].astype(f32)) for j in js]
        mixed = [
            dot(twice(ft[tab[FIRST, j]]), jnp.concatenate(pair, axis=0), AB)
            for j, pair in zip(js, pairs)
        ]
        total = acc[...]
        for j, m in zip(js, mixed):
            total = total + m * second[j].astype(f32)
        acc[...] = total
        return carry

    lax.fori_loop(0, second.shape[0] // group, step, 0)
    chunk = row_sums(acc[...] * (1.0 / 128.0))
    lanes = iota((2, 128), 1) + 128 * (1 - iota((2, 128), 0))
    for j in range(second.shape[0]):
        chunk = jnp.where(lanes == SPARE + j, tab[SERVED, j].astype(f32), chunk)
    for i in range(out.shape[0]):
        out[i] = chunk


def sum_kernel(parts, out, served):
    total = total_of(parts)
    for i in range(out.shape[0]):
        out[i] = total
    n_x = served.shape[0]
    near = parts[pl.ds(lax.axis_index(GRP) * n_x, n_x)]
    lanes = iota((1, 128), 1)
    mine = (lanes >= SPARE) & (lanes < SPARE + 16)
    for i in range(n_x):
        served[i : i + 1] = jnp.where(mine, near[i, 1:2], 0.0).astype(jnp.int32)


def total_of(parts):
    total = parts[0]
    for i in range(1, parts.shape[0]):
        total = total + parts[i]
    return total


LEVELS = 32000.0
OCTAVE = 64.0


def exponent(peak):
    return jnp.ceil(OCTAVE * jnp.log2(jnp.maximum(peak, 1e-30)))


def scale_of(k):
    return jnp.exp2(k * (1.0 / OCTAVE))


def whole(x):
    return jnp.round(x).astype(jnp.int32).astype(jnp.int16)


def real(x):
    return x.astype(jnp.int32).astype(f32)


def peaks(x):
    return jnp.max(jnp.abs(x), axis=1, keepdims=True)


def iota(dims, axis):
    return lax.broadcasted_iota(jnp.int32, dims, axis)


def tile_of(height, pieces):
    used = sum(p.shape[0] for p in pieces)
    return jnp.concatenate(pieces + [jnp.zeros((height - used, 128), f32)], axis=0)


def digits(pair):
    k = exponent(jnp.max(peaks(pair), axis=0, keepdims=True))
    wide = pair * (LEVELS * scale_of(-k))
    high = jnp.round(wide)
    return [high, (wide - high) * LEVELS, jnp.broadcast_to(k, (1, 128))]


def undigit(tile, at):
    s = scale_of(tile[at + 4 : at + 5]) * (1.0 / LEVELS)
    return s * (tile[at : at + 2] + tile[at + 2 : at + 4] * (1.0 / LEVELS))


def undigits(tiles, at):
    total = undigit(tiles[0], at)
    for t in tiles[1:]:
        total = total + undigit(t, at)
    return total


def upright(rows, height):
    tall = jnp.concatenate(rows + [jnp.zeros((128 - len(rows), 128), f32)], axis=0)
    return jnp.transpose(tall)[:height]


def terms_kernel(
    scale, rate, tab, ft, second, mats, sums, labels,
    out_hbm, own_hbm, to_1, to_2, to_3, acc, errs, stash, tops, dense, out, to_all, sems,
):
    samples = second.shape[1]
    n_x, size = dense.shape[0], dense.shape[1]
    rows, parts = samples // n_x, size // 128
    errors = jax.nn.sigmoid(scale * total_of(sums)) - labels[...]
    errs[...] = spread(errors, samples)
    acc[...] = jnp.zeros_like(acc)
    dense[...] = jnp.zeros_like(dense)
    tops[...] = jnp.zeros_like(tops)
    lanes = iota((samples, 128), 1)

    group = math.gcd(TERMS_GROUP, second.shape[0])

    def step(q, carry):
        js = [q * group + i for i in range(group)]
        lives = [tab[LIVE, j].astype(f32) for j in js]
        slots = [tab[SLOT, j] for j in js]
        firsts = [tab[FIRST, j] for j in js]
        vas, vbs = [ft[first] for first in firsts], [second[j] for j in js]
        e = errs[...]
        both = [dot(va, beside(vb.astype(f32) * e), ATB) for va, vb in zip(vas, vbs)]
        updated = [
            (mats[slot] - (rate * live) * (g[:, :128] + g[:, 128:])) * live
            for slot, live, g in zip(slots, lives, both)
        ]
        pairs = [split(m) for m in updated]
        mixed = [
            dot(twice(va), jnp.concatenate(pair, axis=0), AB) for va, pair in zip(vas, pairs)
        ]
        toward = [
            dot(twice(vb), jnp.concatenate(pair, axis=1), ABT) for vb, pair in zip(vbs, pairs)
        ]
        total, top = acc[...], tops[...]
        for j, m, vb in zip(js, mixed, vbs):
            stash[j] = m
            total = total + m * vb.astype(f32)
            top = jnp.where(lanes == j, peaks(m), top)
        acc[...] = total
        tops[...] = top
        for first, t in zip(firsts, toward):
            at = pl.ds(pl.multiple_of(first * rows, 8), rows)
            for i in range(n_x):
                dense[i, at] += t[i * rows : (i + 1) * rows]
        return carry

    lax.fori_loop(0, second.shape[0] // group, step, 0)

    x = tab[MY_X, 0]
    copies = [pltpu.make_async_copy(dense.at[x], own_hbm, sems.at[0])]
    copies[0].start()
    lanes = iota((128, 128), 1)
    far = [lax.rem(x + r, n_x) for r in range(1, n_x)]
    high = jnp.zeros((128, 128), f32)
    for i, to in enumerate(far):
        for t in range(parts):
            top = peaks(dense[to, t * 128 : (t + 1) * 128])
            high = jnp.where(lanes == i * parts + t, top, high)
    k = exponent(high)
    up = LEVELS * scale_of(-k)
    lying = jnp.transpose(k)
    for i, (to, ref) in enumerate(zip(far, (to_1, to_2, to_3))):
        for t in range(parts):
            lane = i * parts + t
            part = dense[to, t * 128 : (t + 1) * 128]
            to_all[i, t * 128 : (t + 1) * 128] = whole(part * up[:, lane : lane + 1])
        mine = lying[i * parts : (i + 1) * parts]
        to_all[i, size : size + 8] = whole(tile_of(8, [mine]))
        copies.append(pltpu.make_async_copy(to_all.at[i], ref, sems.at[1 + i]))
        copies[-1].start()

    k = exponent(tops[...])
    up = LEVELS * scale_of(-k)
    zero = jnp.zeros((1, 128), f32)
    tail = tile_of(8, [zero] + digits(row_sums(acc[...] * (1.0 / 128.0))))
    top_row = iota((8, 128), 0) == 0
    for i in range(n_x):
        part = slice(i * rows, (i + 1) * rows)
        lying = jnp.transpose(tile_of(128, [k[part]]))
        for j in range(second.shape[0]):
            d = j * n_x + i
            out[d, 0:rows] = whole(stash[j, part] * up[part, j : j + 1])
            out[d, rows : rows + 8] = whole(jnp.where(top_row, lying[j : j + 1], tail))

    copies.append(pltpu.make_async_copy(out, out_hbm, sems.at[n_x]))
    copies[-1].start()
    for copy in copies:
        copy.wait()


def across_kernel(served, got, own, from_1, from_2, from_3, out, sums, parted):
    n_x, n_z = served.shape[0], out.shape[0]
    wide = out.shape[1] - 16
    few = wide // 16
    size, rows = own.shape[0], n_z * few
    parts = size // 128

    sides = (from_1, from_2, from_3)
    exps = [real(ref[size : size + 8])[0:parts] for ref in sides]
    down = jnp.transpose(tile_of(128, exps))
    down = scale_of(down) * (1.0 / LEVELS)
    for t in range(parts):
        part = slice(t * 128, (t + 1) * 128)
        total = own[part]
        for i, ref in enumerate(sides):
            lane = i * parts + t
            total = total + real(ref[part]) * down[:, lane : lane + 1]
        sums[part] = total

    tiles = [real(got[d, rows : rows + 8]) for d in range(got.shape[0])]
    down = scale_of(upright([t[0:1] for t in tiles], rows)) * (1.0 / LEVELS)
    for q in range(0, got.shape[0], 8):
        values = [real(got[d, 0:rows]) * down[:, d : d + 1] for d in range(q, q + 8)]
        for d, value in zip(range(q, q + 8), values):
            field = served[d % n_x, SPARE + d // n_x]
            at = pl.ds(pl.multiple_of(field * rows, 8), rows)
            sums[at] += value
    for f in range(16):
        for z in range(n_z):
            start = f * rows + z * few
            parted[z, f * few : (f + 1) * few] = sums[start : start + few]
    lanes = iota((wide, 128), 1)
    tops = jnp.zeros((wide, 128), f32)
    for z in range(n_z):
        tops = jnp.where(lanes == z, peaks(parted[z]), tops)
    k = exponent(tops)
    up = LEVELS * scale_of(-k)
    if wide < 128:
        k = tile_of(128, [k])
    lying = [jnp.transpose(k[n * 128 : (n + 1) * 128]) for n in range(k.shape[0] // 128)]
    common = digits(undigits(tiles, 1))
    for z in range(n_z):
        out[z, 0:wide] = whole(parted[z] * up[:, z : z + 1])
        mine = [part[z : z + 1] for part in lying]
        out[z, wide : wide + 16] = whole(tile_of(16, mine + common))


def last_kernel(
    scale, rate, tab, ft, second, mats_in, got, first_sums, labels, logits, grads, mats, errs, sums
):
    samples = second.shape[1]
    few = grads.shape[0]
    wide = 16 * few
    tiles = [real(got[i, wide : wide + 16]) for i in range(got.shape[0])]
    high = -(-wide // 128)
    exps = [upright([t[n : n + 1] for t in tiles], min(wide, 128)) for n in range(high)]
    down = scale_of(jnp.concatenate(exps, axis=0)) * (1.0 / LEVELS)
    value = scale * undigits(tiles, high)
    logits[...] = value
    errors = jax.nn.sigmoid(value) - labels[...]
    errs[...] = spread(errors, samples)
    total = real(got[0, 0:wide]) * down[:, 0:1]
    for i in range(1, got.shape[0]):
        total = total + real(got[i, 0:wide]) * down[:, i : i + 1]
    sums[...] = total * (1.0 / math.sqrt(128.0))
    for b in range(few):
        mine = errs[pl.ds(tab[MY_OWN, 0] * few + b, 1)]
        grads[b] = sums[pl.ds(b, 16, stride=few)] * mine
    earlier = jax.nn.sigmoid(scale * total_of(first_sums)) - labels[...]
    errs[...] = spread(errors + earlier, samples)

    group = math.gcd(LAST_GROUP, second.shape[0])

    def step(q, carry):
        js = [q * group + i for i in range(group)]
        e = errs[...]
        both = [dot(ft[tab[FIRST, j]], beside(second[j].astype(f32) * e), ATB) for j in js]
        for j, g in zip(js, both):
            slot, live = tab[SLOT, j], tab[LIVE, j].astype(f32)
            mats[slot] = mats_in[slot] - (rate * live) * (g[:, :128] + g[:, 128:])
        return carry

    lax.fori_loop(0, second.shape[0] // group, step, 0)


def call(kernel, outs, n_in, scratch=(), smem=True, far_out=False, room=16):
    specs = [pl.BlockSpec(memory_space=pltpu.VMEM)] * n_in
    if smem:
        specs[0] = pl.BlockSpec(memory_space=pltpu.SMEM)
    space = pltpu.HBM if far_out else pltpu.VMEM
    return pl.pallas_call(
        kernel,
        out_shape=outs,
        in_specs=specs,
        out_specs=[pl.BlockSpec(memory_space=space)] * len(outs),
        scratch_shapes=list(scratch),
        compiler_params=pltpu.CompilerParams(vmem_limit_bytes=room << 20),
    )


def shape(dims, dtype=f32):
    return jax.ShapeDtypeStruct(dims, dtype)


def swap(x, axes):
    return lax.all_to_all(x, axes, split_axis=0, concat_axis=0, tiled=True)


def on_device(fields, labels, pair_first, pair_second, pair_count, pair_mats):
    groups, owners = lax.axis_size(GRP), lax.axis_size(OWN)
    n_x, n_z = lax.axis_size("x"), lax.axis_size("z")
    me = lax.axis_index(GRP)
    samples, per_block, feature = fields.shape
    slots = pair_first.shape[2]
    scale = logit_gain / math.sqrt(groups * owners * slots)
    rate = step_size * scale / (samples * feature)
    few = samples // owners

    table = pair_second[:, 0, :]
    blocks = table // per_block
    served = jnp.sum(jnp.where(blocks == me, table - me * per_block, 0), axis=1)
    mine = lax.dynamic_index_in_dim(blocks, me, 0, keepdims=False)
    picked = mine[:, None] == jnp.arange(slots, dtype=jnp.int32)[None, :]
    slot_ids = jnp.arange(slots, dtype=jnp.int32)[:, None]
    slot_of = jnp.sum(jnp.where(picked, slot_ids, 0), axis=0)
    first_of = jnp.sum(jnp.where(picked, (pair_first[0, 0] - me * per_block)[:, None], 0), axis=0)
    live = (slot_of < pair_count[0, 0]).astype(jnp.int32)
    places = [lax.axis_index(OWN), lax.axis_index("x")]
    places = [jnp.full((slots,), place, jnp.int32) for place in places]
    tab = jnp.stack([slot_of, first_of, live, served] + places)

    ft = jnp.transpose(fields, (1, 0, 2))
    mats = pair_mats[0, 0]
    targets = jnp.pad(labels.astype(f32), (0, 256 - samples)).reshape(2, 128)

    sent = call(gather_kernel, [shape((slots, samples, feature), bf16)], 2)(tab, ft)[0]
    sent, targets = lax.optimization_barrier((sent, targets))
    second = swap(sent, GRP)
    acc = pltpu.VMEM((samples, 128), f32)
    part = call(partial_kernel, [shape((groups * n_x, 2, 128))], 4, [acc])(tab, ft, second, mats)[0]
    out = [shape((n_z, 2, 128)), shape((n_x, 128), jnp.int32)]
    part, near = call(sum_kernel, out, 1, smem=False)(swap(part, GRP + ("x",)))
    sums = swap(part, "z")

    rows, wide = samples // n_x, per_block * few
    size = per_block * rows
    side = shape((size + 8, feature), jnp.int16)
    out, own, *sides = call(
        functools.partial(terms_kernel, scale, rate),
        [
            shape((groups * n_x, rows + 8, feature), jnp.int16),
            shape((size, feature)),
            side,
            side,
            side,
        ],
        6,
        [
            acc,
            acc,
            pltpu.VMEM((slots, samples, feature), f32),
            acc,
            pltpu.VMEM((n_x, size, feature), f32),
            pltpu.VMEM((groups * n_x, rows + 8, feature), jnp.int16),
            pltpu.VMEM((n_x - 1, size + 8, feature), jnp.int16),
            pltpu.SemaphoreType.DMA((n_x + 1,)),
        ],
        far_out=True,
        room=60,
    )(tab, ft, second, mats, sums, targets)
    got = swap(out, GRP + ("x",))
    sides = [
        lax.ppermute(side, "x", [(i, (i + r) % n_x) for i in range(n_x)])
        for r, side in enumerate(sides, 1)
    ]
    out = [shape((n_z, wide + 16, feature), jnp.int16)]
    room = [pltpu.VMEM((size, feature), f32), pltpu.VMEM((n_z, wide, feature), f32)]
    got = call(across_kernel, out, 6, room, room=16)(near, got, own, *sides)[0]
    got = swap(got, "z")
    logits, grads, mats = call(
        functools.partial(last_kernel, scale, rate),
        [shape((2, 128)), shape((few, per_block, feature)), shape(mats.shape)],
        7,
        [acc, pltpu.VMEM((per_block * few, 128), f32)],
    )(tab, ft, second, mats, got, sums, targets)
    return logits.reshape(256)[:samples], grads, mats[None, None]


def solution(mesh):
    n_grp, n_own = mesh.devices.shape
    sizes = (n_grp // 2, 2, 4, n_own // 4)
    split_mesh = Mesh(mesh.devices.reshape(sizes), ("y", "core", "x", "z"))
    in_specs = (
        P(None, GRP, None),
        P(),
        P(GRP, OWN, None),
        P(None, OWN, None),
        P(GRP, OWN),
        P(GRP, OWN, None, None, None),
    )
    out_specs = (P(), P(OWN, GRP, None), P(GRP, OWN, None, None, None))
    return jax.shard_map(
        on_device, mesh=split_mesh, in_specs=in_specs, out_specs=out_specs, check_vma=False
    )
```

```python
import functools
import math

import jax
import jax.numpy as jnp
from jax import lax
from jax.experimental import pallas as pl
from jax.experimental.pallas import tpu as pltpu
from jax.sharding import Mesh
from jax.sharding import PartitionSpec as P

GRP = ("y", "core")
OWN = ("x", "z")
logit_gain = 1.5
step_size = 1000.0
f32 = jnp.float32
bf16 = jnp.bfloat16

SLOT, FIRST, LIVE, SERVED, MY_OWN, MY_X = range(6)

PARTIAL_GROUP, TERMS_GROUP, LAST_GROUP = 16, 16, 16
SPARE = 64


def split(x):
    hi = x.astype(bf16)
    return hi, (x - hi.astype(f32)).astype(bf16)


def dot(a, b, dims):
    return lax.dot_general(a, b, (dims, ((), ())), preferred_element_type=f32)


def beside(x):
    return jnp.concatenate(split(x), axis=1)


def twice(x):
    return jnp.concatenate([x, x], axis=1)


AB, ABT, ATB = ((1,), (0,)), ((1,), (1,)), ((0,), (0,))


def row_sums(acc):
    ones = jnp.ones((8, 128), f32)
    exact = functools.partial(
        lax.dot_general,
        dimension_numbers=(ABT, ((), ())),
        precision=lax.Precision.HIGHEST,
        preferred_element_type=f32,
    )
    low = exact(ones, acc[:128])
    rest = acc[128:]
    high = exact(ones, jnp.concatenate([rest, jnp.zeros((256 - acc.shape[0], 128), f32)], axis=0))
    return jnp.concatenate([low[0:1], high[0:1]], axis=0)


def spread(chunk, samples):
    low = jnp.transpose(jnp.broadcast_to(chunk[0:1], (128, 128)))
    high = jnp.transpose(jnp.broadcast_to(chunk[1:2], (128, 128)))
    return jnp.concatenate([low, high[: samples - 128]], axis=0)


def gather_kernel(tab, ft, out):
    @pl.loop(0, out.shape[0])
    def _(j):
        out[j] = ft[tab[SERVED, j]]


def partial_kernel(tab, ft, second, mats, out, acc):
    acc[...] = jnp.zeros_like(acc)

    group = math.gcd(PARTIAL_GROUP, second.shape[0])

    def step(q, carry):
        js = [q * group + i for i in range(group)]
        pairs = [split(mats[tab[SLOT, j]] * tab[LIVE, j].astype(f32)) for j in js]
        mixed = [
            dot(twice(ft[tab[FIRST, j]]), jnp.concatenate(pair, axis=0), AB)
            for j, pair in zip(js, pairs)
        ]
        total = acc[...]
        for j, m in zip(js, mixed):
            total = total + m * second[j].astype(f32)
        acc[...] = total
        return carry

    lax.fori_loop(0, second.shape[0] // group, step, 0)
    chunk = row_sums(acc[...] * (1.0 / 128.0))
    lanes = iota((2, 128), 1) + 128 * (1 - iota((2, 128), 0))
    for j in range(second.shape[0]):
        chunk = jnp.where(lanes == SPARE + j, tab[SERVED, j].astype(f32), chunk)
    for i in range(out.shape[0]):
        out[i] = chunk


def sum_kernel(parts, out, served):
    total = total_of(parts)
    for i in range(out.shape[0]):
        out[i] = total
    n_x = served.shape[0]
    near = parts[pl.ds(lax.axis_index(GRP) * n_x, n_x)]
    lanes = iota((1, 128), 1)
    mine = (lanes >= SPARE) & (lanes < SPARE + 16)
    for i in range(n_x):
        served[i : i + 1] = jnp.where(mine, near[i, 1:2], 0.0).astype(jnp.int32)


def folded(labels):
    row = labels[...].astype(f32)
    rest = jnp.zeros((1, 256 - row.shape[1]), f32)
    return jnp.concatenate([row[:, :128], jnp.concatenate([row[:, 128:], rest], axis=1)], axis=0)


def total_of(parts):
    total = parts[0]
    for i in range(1, parts.shape[0]):
        total = total + parts[i]
    return total


LEVELS = 32000.0
OCTAVE = 64.0


def exponent(peak):
    return jnp.ceil(OCTAVE * jnp.log2(jnp.maximum(peak, 1e-30)))


def scale_of(k):
    return jnp.exp2(k * (1.0 / OCTAVE))


def whole(x):
    return jnp.round(x).astype(jnp.int32).astype(jnp.int16)


def real(x):
    return x.astype(jnp.int32).astype(f32)


def peaks(x):
    return jnp.max(jnp.abs(x), axis=1, keepdims=True)


def iota(dims, axis):
    return lax.broadcasted_iota(jnp.int32, dims, axis)


def tile_of(height, pieces):
    used = sum(p.shape[0] for p in pieces)
    return jnp.concatenate(pieces + [jnp.zeros((height - used, 128), f32)], axis=0)


def digits(pair):
    k = exponent(jnp.max(peaks(pair), axis=0, keepdims=True))
    wide = pair * (LEVELS * scale_of(-k))
    high = jnp.round(wide)
    return [high, (wide - high) * LEVELS, jnp.broadcast_to(k, (1, 128))]


def undigit(tile, at):
    s = scale_of(tile[at + 4 : at + 5]) * (1.0 / LEVELS)
    return s * (tile[at : at + 2] + tile[at + 2 : at + 4] * (1.0 / LEVELS))


def undigits(tiles, at):
    total = undigit(tiles[0], at)
    for t in tiles[1:]:
        total = total + undigit(t, at)
    return total


def upright(rows, height):
    tall = jnp.concatenate(rows + [jnp.zeros((128 - len(rows), 128), f32)], axis=0)
    return jnp.transpose(tall)[:height]


def terms_kernel(
    scale, rate, tab, ft_hbm, second_hbm, mats_hbm, sums, labels,
    out_hbm, own_hbm, to_1, to_2, to_3,
    acc, errs, stash, tops, dense, out, to_all, ft, second, mats, sems, load_sems,
):
    loads = [
        pltpu.make_async_copy(far, near, load_sems.at[i])
        for i, (far, near) in enumerate(((ft_hbm, ft), (second_hbm, second), (mats_hbm, mats)))
    ]
    for load in loads:
        load.start()
    samples = second.shape[1]
    n_x, size = dense.shape[0], dense.shape[1]
    rows, parts = samples // n_x, size // 128
    errors = jax.nn.sigmoid(scale * total_of(sums)) - folded(labels)
    errs[...] = spread(errors, samples)
    acc[...] = jnp.zeros_like(acc)
    dense[...] = jnp.zeros_like(dense)
    tops[...] = jnp.zeros_like(tops)
    lanes = iota((samples, 128), 1)

    for load in loads:
        load.wait()

    group = math.gcd(TERMS_GROUP, second.shape[0])

    def step(q, carry):
        js = [q * group + i for i in range(group)]
        lives = [tab[LIVE, j].astype(f32) for j in js]
        slots = [tab[SLOT, j] for j in js]
        firsts = [tab[FIRST, j] for j in js]
        vas, vbs = [ft[first] for first in firsts], [second[j] for j in js]
        e = errs[...]
        both = [dot(va, beside(vb.astype(f32) * e), ATB) for va, vb in zip(vas, vbs)]
        updated = [
            (mats[slot] - (rate * live) * (g[:, :128] + g[:, 128:])) * live
            for slot, live, g in zip(slots, lives, both)
        ]
        pairs = [split(m) for m in updated]
        mixed = [
            dot(twice(va), jnp.concatenate(pair, axis=0), AB) for va, pair in zip(vas, pairs)
        ]
        toward = [
            dot(twice(vb), jnp.concatenate(pair, axis=1), ABT) for vb, pair in zip(vbs, pairs)
        ]
        total, top = acc[...], tops[...]
        for j, m, vb in zip(js, mixed, vbs):
            stash[j] = m
            total = total + m * vb.astype(f32)
            top = jnp.where(lanes == j, peaks(m), top)
        acc[...] = total
        tops[...] = top
        for first, t in zip(firsts, toward):
            at = pl.ds(pl.multiple_of(first * rows, 8), rows)
            for i in range(n_x):
                dense[i, at] += t[i * rows : (i + 1) * rows]
        return carry

    lax.fori_loop(0, second.shape[0] // group, step, 0)

    x = tab[MY_X, 0]
    copies = [pltpu.make_async_copy(dense.at[x], own_hbm, sems.at[0])]
    copies[0].start()
    lanes = iota((128, 128), 1)
    far = [lax.rem(x + r, n_x) for r in range(1, n_x)]
    high = jnp.zeros((128, 128), f32)
    for i, to in enumerate(far):
        for t in range(parts):
            top = peaks(dense[to, t * 128 : (t + 1) * 128])
            high = jnp.where(lanes == i * parts + t, top, high)
    k = exponent(high)
    up = LEVELS * scale_of(-k)
    lying = jnp.transpose(k)
    for i, (to, ref) in enumerate(zip(far, (to_1, to_2, to_3))):
        for t in range(parts):
            lane = i * parts + t
            part = dense[to, t * 128 : (t + 1) * 128]
            to_all[i, t * 128 : (t + 1) * 128] = whole(part * up[:, lane : lane + 1])
        mine = lying[i * parts : (i + 1) * parts]
        to_all[i, size : size + 8] = whole(tile_of(8, [mine]))
        copies.append(pltpu.make_async_copy(to_all.at[i], ref, sems.at[1 + i]))
        copies[-1].start()

    k = exponent(tops[...])
    up = LEVELS * scale_of(-k)
    zero = jnp.zeros((1, 128), f32)
    tail = tile_of(8, [zero] + digits(row_sums(acc[...] * (1.0 / 128.0))))
    top_row = iota((8, 128), 0) == 0
    lying = [jnp.transpose(tile_of(128, [k[i * rows : (i + 1) * rows]])) for i in range(n_x)]
    quarter = max(1, second.shape[0] // 4)
    for q in range(0, second.shape[0], quarter):
        for j in range(q, q + quarter):
            for i in range(n_x):
                d, part = j * n_x + i, slice(i * rows, (i + 1) * rows)
                out[d, 0:rows] = whole(stash[j, part] * up[part, j : j + 1])
                out[d, rows : rows + 8] = whole(jnp.where(top_row, lying[i][j : j + 1], tail))
        piece = slice(q * n_x, (q + quarter) * n_x)
        sem = sems.at[n_x + q // quarter]
        copies.append(pltpu.make_async_copy(out.at[piece], out_hbm.at[piece], sem))
        copies[-1].start()
    for copy in copies:
        copy.wait()


def across_kernel(served, got, own, from_1, from_2, from_3, out, sums, parted):
    n_x, n_z = served.shape[0], out.shape[0]
    wide = out.shape[1] - 8
    few = wide // 16
    size, rows = own.shape[0], n_z * few
    parts = size // 128

    sides = (from_1, from_2, from_3)
    exps = [real(ref[size : size + 8])[0:parts] for ref in sides]
    down = jnp.transpose(tile_of(128, exps))
    down = scale_of(down) * (1.0 / LEVELS)
    for t in range(parts):
        part = slice(t * 128, (t + 1) * 128)
        total = own[part]
        for i, ref in enumerate(sides):
            lane = i * parts + t
            total = total + real(ref[part]) * down[:, lane : lane + 1]
        sums[part] = total

    tiles = [real(got[d, rows : rows + 8]) for d in range(got.shape[0])]
    down = scale_of(upright([t[0:1] for t in tiles], rows)) * (1.0 / LEVELS)
    for q in range(0, got.shape[0], 8):
        values = [real(got[d, 0:rows]) * down[:, d : d + 1] for d in range(q, q + 8)]
        for d, value in zip(range(q, q + 8), values):
            field = served[d % n_x, SPARE + d // n_x]
            at = pl.ds(pl.multiple_of(field * rows, 8), rows)
            sums[at] += value
    for f in range(16):
        for z in range(n_z):
            start = f * rows + z * few
            parted[z, f * few : (f + 1) * few] = sums[start : start + few]
    lanes = iota((wide, 128), 1)
    tops = jnp.zeros((wide, 128), f32)
    for z in range(n_z):
        tops = jnp.where(lanes == z, peaks(parted[z]), tops)
    k = exponent(tops)
    up = LEVELS * scale_of(-k)
    if wide < 128:
        k = tile_of(128, [k])
    lying = [jnp.transpose(k[n * 128 : (n + 1) * 128]) for n in range(k.shape[0] // 128)]
    common = digits(undigits(tiles, 1))
    for z in range(n_z):
        out[z, 0:wide] = whole(parted[z] * up[:, z : z + 1])
        mine = [part[z : z + 1] for part in lying]
        out[z, wide : wide + 8] = whole(tile_of(8, mine + common))


def last_kernel(
    scale, rate, tab, ft, second, mats_in, got, first_sums, labels, logits, grads, mats, errs, sums
):
    samples = second.shape[1]
    few = grads.shape[0]
    wide = 16 * few
    tiles = [real(got[i, wide : wide + 8]) for i in range(got.shape[0])]
    high = -(-wide // 128)
    exps = [upright([t[n : n + 1] for t in tiles], min(wide, 128)) for n in range(high)]
    down = scale_of(jnp.concatenate(exps, axis=0)) * (1.0 / LEVELS)
    value = scale * undigits(tiles, high)
    logits[...] = value
    targets = folded(labels)
    errors = jax.nn.sigmoid(value) - targets
    errs[...] = spread(errors, samples)
    total = real(got[0, 0:wide]) * down[:, 0:1]
    for i in range(1, got.shape[0]):
        total = total + real(got[i, 0:wide]) * down[:, i : i + 1]
    sums[...] = total * (1.0 / math.sqrt(128.0))
    for b in range(few):
        mine = errs[pl.ds(tab[MY_OWN, 0] * few + b, 1)]
        grads[b] = sums[pl.ds(b, 16, stride=few)] * mine
    earlier = jax.nn.sigmoid(scale * total_of(first_sums)) - targets
    errs[...] = spread(errors + earlier, samples)

    group = math.gcd(LAST_GROUP, second.shape[0])

    def step(q, carry):
        js = [q * group + i for i in range(group)]
        e = errs[...]
        both = [dot(ft[tab[FIRST, j]], beside(second[j].astype(f32) * e), ATB) for j in js]
        for j, g in zip(js, both):
            slot, live = tab[SLOT, j], tab[LIVE, j].astype(f32)
            mats[slot] = mats_in[slot] - (rate * live) * (g[:, :128] + g[:, 128:])
        return carry

    lax.fori_loop(0, second.shape[0] // group, step, 0)


def call(kernel, outs, n_in, scratch=(), smem=True, far_in=(), far_out=False, room=16):
    specs = [pl.BlockSpec(memory_space=pltpu.VMEM)] * n_in
    if smem:
        specs[0] = pl.BlockSpec(memory_space=pltpu.SMEM)
    for i in far_in:
        specs[i] = pl.BlockSpec(memory_space=pltpu.HBM)
    space = pltpu.HBM if far_out else pltpu.VMEM
    return pl.pallas_call(
        kernel,
        out_shape=outs,
        in_specs=specs,
        out_specs=[pl.BlockSpec(memory_space=space)] * len(outs),
        scratch_shapes=list(scratch),
        compiler_params=pltpu.CompilerParams(vmem_limit_bytes=room << 20),
    )


def shape(dims, dtype=f32):
    return jax.ShapeDtypeStruct(dims, dtype)


def swap(x, axes):
    return lax.all_to_all(x, axes, split_axis=0, concat_axis=0, tiled=True)


def on_device(fields, labels, pair_first, pair_second, pair_count, pair_mats):
    groups, owners = lax.axis_size(GRP), lax.axis_size(OWN)
    n_x, n_z = lax.axis_size("x"), lax.axis_size("z")
    me = lax.axis_index(GRP)
    samples, per_block, feature = fields.shape
    slots = pair_first.shape[2]
    scale = logit_gain / math.sqrt(groups * owners * slots)
    rate = step_size * scale / (samples * feature)
    few = samples // owners

    table = pair_second[:, 0, :]
    blocks = table // per_block
    served = jnp.sum(jnp.where(blocks == me, table - me * per_block, 0), axis=1)
    mine = lax.dynamic_index_in_dim(blocks, me, 0, keepdims=False)
    picked = mine[:, None] == jnp.arange(slots, dtype=jnp.int32)[None, :]
    slot_ids = jnp.arange(slots, dtype=jnp.int32)[:, None]
    slot_of = jnp.sum(jnp.where(picked, slot_ids, 0), axis=0)
    first_of = jnp.sum(jnp.where(picked, (pair_first[0, 0] - me * per_block)[:, None], 0), axis=0)
    live = (slot_of < pair_count[0, 0]).astype(jnp.int32)
    places = [lax.axis_index(OWN), lax.axis_index("x")]
    places = [jnp.full((slots,), place, jnp.int32) for place in places]
    tab = jnp.stack([slot_of, first_of, live, served] + places)

    ft = jnp.transpose(fields, (1, 0, 2))
    mats = pair_mats[0, 0]
    targets = labels.reshape(1, samples)

    sent = call(gather_kernel, [shape((slots, samples, feature), bf16)], 2)(tab, ft)[0]
    second = swap(sent, GRP)
    acc = pltpu.VMEM((samples, 128), f32)
    part = call(partial_kernel, [shape((groups * n_x, 2, 128))], 4, [acc])(tab, ft, second, mats)[0]
    out = [shape((n_z, 2, 128)), shape((n_x, 128), jnp.int32)]
    part, near = call(sum_kernel, out, 1, smem=False)(swap(part, GRP + ("x",)))
    sums = swap(part, "z")

    rows, wide = samples // n_x, per_block * few
    size = per_block * rows
    side = shape((size + 8, feature), jnp.int16)
    out, own, *sides = call(
        functools.partial(terms_kernel, scale, rate),
        [
            shape((groups * n_x, rows + 8, feature), jnp.int16),
            shape((size, feature)),
            side,
            side,
            side,
        ],
        6,
        [
            acc,
            acc,
            pltpu.VMEM((slots, samples, feature), f32),
            acc,
            pltpu.VMEM((n_x, size, feature), f32),
            pltpu.VMEM((groups * n_x, rows + 8, feature), jnp.int16),
            pltpu.VMEM((n_x - 1, size + 8, feature), jnp.int16),
            pltpu.VMEM(ft.shape, bf16),
            pltpu.VMEM(second.shape, bf16),
            pltpu.VMEM(mats.shape, f32),
            pltpu.SemaphoreType.DMA((n_x + 4,)),
            pltpu.SemaphoreType.DMA((3,)),
        ],
        far_in=(1, 2, 3),
        far_out=True,
        room=60,
    )(tab, ft, second, mats, sums, targets)
    got = swap(out, GRP + ("x",))
    sides = [
        lax.ppermute(side, "x", [(i, (i + r) % n_x) for i in range(n_x)])
        for r, side in enumerate(sides, 1)
    ]
    out = [shape((n_z, wide + 8, feature), jnp.int16)]
    room = [pltpu.VMEM((size, feature), f32), pltpu.VMEM((n_z, wide, feature), f32)]
    got = call(across_kernel, out, 6, room, room=16)(near, got, own, *sides)[0]
    got = swap(got, "z")
    logits, grads, mats = call(
        functools.partial(last_kernel, scale, rate),
        [shape((2, 128)), shape((few, per_block, feature)), shape(mats.shape)],
        7,
        [acc, pltpu.VMEM((per_block * few, 128), f32)],
    )(tab, ft, second, mats, got, sums, targets)
    return logits.reshape(256)[:samples], grads, mats[None, None]


def solution(mesh):
    n_grp, n_own = mesh.devices.shape
    sizes = (n_grp // 2, 2, 4, n_own // 4)
    split_mesh = Mesh(mesh.devices.reshape(sizes), ("y", "core", "x", "z"))
    in_specs = (
        P(None, GRP, None),
        P(),
        P(GRP, OWN, None),
        P(None, OWN, None),
        P(GRP, OWN),
        P(GRP, OWN, None, None, None),
    )
    out_specs = (P(), P(OWN, GRP, None), P(GRP, OWN, None, None, None))
    return jax.shard_map(
        on_device, mesh=split_mesh, in_specs=in_specs, out_specs=out_specs, check_vma=False
    )
```

```python
import functools
import math

import jax
import jax.numpy as jnp
from jax import lax
from jax.experimental import pallas as pl
from jax.experimental.pallas import tpu as pltpu
from jax.sharding import Mesh
from jax.sharding import PartitionSpec as P

GRP = ("y", "core")
OWN = ("x", "z")
logit_gain = 1.5
step_size = 1000.0
f32 = jnp.float32
bf16 = jnp.bfloat16

SLOT, FIRST, LIVE, SERVED, MY_OWN, MY_X = range(6)

PARTIAL_GROUP, TERMS_GROUP, LAST_GROUP = 16, 16, 16
SPARE = 64


def split(x):
    hi = x.astype(bf16)
    return hi, (x - hi.astype(f32)).astype(bf16)


def dot(a, b, dims):
    return lax.dot_general(a, b, (dims, ((), ())), preferred_element_type=f32)


def beside(x):
    return jnp.concatenate(split(x), axis=1)


def twice(x):
    return jnp.concatenate([x, x], axis=1)


AB, ABT, ATB = ((1,), (0,)), ((1,), (1,)), ((0,), (0,))


def row_sums(acc):
    ones = jnp.ones((8, 128), f32)
    exact = functools.partial(
        lax.dot_general,
        dimension_numbers=(ABT, ((), ())),
        precision=lax.Precision.HIGHEST,
        preferred_element_type=f32,
    )
    low = exact(ones, acc[:128])
    rest = acc[128:]
    high = exact(ones, jnp.concatenate([rest, jnp.zeros((256 - acc.shape[0], 128), f32)], axis=0))
    return jnp.concatenate([low[0:1], high[0:1]], axis=0)


def spread(chunk, samples):
    low = jnp.transpose(jnp.broadcast_to(chunk[0:1], (128, 128)))
    high = jnp.transpose(jnp.broadcast_to(chunk[1:2], (128, 128)))
    return jnp.concatenate([low, high[: samples - 128]], axis=0)


def gather_kernel(tab, ft, out):
    @pl.loop(0, out.shape[0])
    def _(j):
        out[j] = ft[tab[SERVED, j]]


def partial_kernel(tab, ft, second, mats, labels_hbm, out, targets, acc, labels, sem):
    load = pltpu.make_async_copy(labels_hbm, labels, sem)
    load.start()
    acc[...] = jnp.zeros_like(acc)

    group = math.gcd(PARTIAL_GROUP, second.shape[0])

    def step(q, carry):
        js = [q * group + i for i in range(group)]
        pairs = [split(mats[tab[SLOT, j]] * tab[LIVE, j].astype(f32)) for j in js]
        mixed = [
            dot(twice(ft[tab[FIRST, j]]), jnp.concatenate(pair, axis=0), AB)
            for j, pair in zip(js, pairs)
        ]
        total = acc[...]
        for j, m in zip(js, mixed):
            total = total + m * second[j].astype(f32)
        acc[...] = total
        return carry

    lax.fori_loop(0, second.shape[0] // group, step, 0)
    chunk = row_sums(acc[...] * (1.0 / 128.0))
    lanes = iota((2, 128), 1) + 128 * (1 - iota((2, 128), 0))
    for j in range(second.shape[0]):
        chunk = jnp.where(lanes == SPARE + j, tab[SERVED, j].astype(f32), chunk)
    for i in range(out.shape[0]):
        out[i] = chunk
    load.wait()
    targets[...] = folded(labels)


def sum_kernel(parts, out, served):
    total = total_of(parts)
    for i in range(out.shape[0]):
        out[i] = total
    n_x = served.shape[0]
    near = parts[pl.ds(lax.axis_index(GRP) * n_x, n_x)]
    lanes = iota((1, 128), 1)
    mine = (lanes >= SPARE) & (lanes < SPARE + 16)
    for i in range(n_x):
        served[i : i + 1] = jnp.where(mine, near[i, 1:2], 0.0).astype(jnp.int32)


def folded(labels):
    row = labels[...].astype(f32)
    rest = jnp.zeros((1, 256 - row.shape[1]), f32)
    return jnp.concatenate([row[:, :128], jnp.concatenate([row[:, 128:], rest], axis=1)], axis=0)


def total_of(parts):
    total = parts[0]
    for i in range(1, parts.shape[0]):
        total = total + parts[i]
    return total


LEVELS = 32000.0
OCTAVE = 64.0


def exponent(peak):
    return jnp.ceil(OCTAVE * jnp.log2(jnp.maximum(peak, 1e-30)))


def scale_of(k):
    return jnp.exp2(k * (1.0 / OCTAVE))


def whole(x):
    return jnp.round(x).astype(jnp.int32).astype(jnp.int16)


def real(x):
    return x.astype(jnp.int32).astype(f32)


def peaks(x):
    return jnp.max(jnp.abs(x), axis=1, keepdims=True)


def iota(dims, axis):
    return lax.broadcasted_iota(jnp.int32, dims, axis)


def tile_of(height, pieces):
    used = sum(p.shape[0] for p in pieces)
    return jnp.concatenate(pieces + [jnp.zeros((height - used, 128), f32)], axis=0)


def digits(pair):
    k = exponent(jnp.max(peaks(pair), axis=0, keepdims=True))
    wide = pair * (LEVELS * scale_of(-k))
    high = jnp.round(wide)
    return [high, (wide - high) * LEVELS, jnp.broadcast_to(k, (1, 128))]


def undigit(tile, at):
    s = scale_of(tile[at + 4 : at + 5]) * (1.0 / LEVELS)
    return s * (tile[at : at + 2] + tile[at + 2 : at + 4] * (1.0 / LEVELS))


def undigits(tiles, at):
    total = undigit(tiles[0], at)
    for t in tiles[1:]:
        total = total + undigit(t, at)
    return total


def upright(rows, height):
    tall = jnp.concatenate(rows + [jnp.zeros((128 - len(rows), 128), f32)], axis=0)
    return jnp.transpose(tall)[:height]


def terms_kernel(
    scale, rate, tab, ft, second, mats, sums, targets,
    out_hbm, own_hbm, to_1, to_2, to_3,
    acc, errs, stash, tops, dense, out, to_all, sems,
):
    samples = second.shape[1]
    n_x, size = dense.shape[0], dense.shape[1]
    rows, parts = samples // n_x, size // 128
    errors = jax.nn.sigmoid(scale * total_of(sums)) - targets[...]
    errs[...] = spread(errors, samples)
    acc[...] = jnp.zeros_like(acc)
    dense[...] = jnp.zeros_like(dense)
    tops[...] = jnp.zeros_like(tops)
    lanes = iota((samples, 128), 1)

    group = math.gcd(TERMS_GROUP, second.shape[0])

    def step(q, carry):
        js = [q * group + i for i in range(group)]
        lives = [tab[LIVE, j].astype(f32) for j in js]
        slots = [tab[SLOT, j] for j in js]
        firsts = [tab[FIRST, j] for j in js]
        vas, vbs = [ft[first] for first in firsts], [second[j] for j in js]
        e = errs[...]
        both = [dot(va, beside(vb.astype(f32) * e), ATB) for va, vb in zip(vas, vbs)]
        updated = [
            (mats[slot] - (rate * live) * (g[:, :128] + g[:, 128:])) * live
            for slot, live, g in zip(slots, lives, both)
        ]
        pairs = [split(m) for m in updated]
        mixed = [
            dot(twice(va), jnp.concatenate(pair, axis=0), AB) for va, pair in zip(vas, pairs)
        ]
        toward = [
            dot(twice(vb), jnp.concatenate(pair, axis=1), ABT) for vb, pair in zip(vbs, pairs)
        ]
        total, top = acc[...], tops[...]
        for j, m, vb in zip(js, mixed, vbs):
            stash[j] = m
            total = total + m * vb.astype(f32)
            top = jnp.where(lanes == j, peaks(m), top)
        acc[...] = total
        tops[...] = top
        for first, t in zip(firsts, toward):
            at = pl.ds(pl.multiple_of(first * rows, 8), rows)
            for i in range(n_x):
                dense[i, at] += t[i * rows : (i + 1) * rows]
        return carry

    lax.fori_loop(0, second.shape[0] // group, step, 0)

    x = tab[MY_X, 0]
    copies = [pltpu.make_async_copy(dense.at[x], own_hbm, sems.at[0])]
    copies[0].start()
    lanes = iota((128, 128), 1)
    far = [lax.rem(x + r, n_x) for r in range(1, n_x)]
    high = jnp.zeros((128, 128), f32)
    for i, to in enumerate(far):
        for t in range(parts):
            top = peaks(dense[to, t * 128 : (t + 1) * 128])
            high = jnp.where(lanes == i * parts + t, top, high)
    k = exponent(high)
    up = LEVELS * scale_of(-k)
    lying = jnp.transpose(k)
    for i, (to, ref) in enumerate(zip(far, (to_1, to_2, to_3))):
        for t in range(parts):
            lane = i * parts + t
            part = dense[to, t * 128 : (t + 1) * 128]
            to_all[i, t * 128 : (t + 1) * 128] = whole(part * up[:, lane : lane + 1])
        mine = lying[i * parts : (i + 1) * parts]
        to_all[i, size : size + 8] = whole(tile_of(8, [mine]))
        copies.append(pltpu.make_async_copy(to_all.at[i], ref, sems.at[1 + i]))
        copies[-1].start()

    k = exponent(tops[...])
    up = LEVELS * scale_of(-k)
    zero = jnp.zeros((1, 128), f32)
    tail = tile_of(8, [zero] + digits(row_sums(acc[...] * (1.0 / 128.0))))
    top_row = iota((8, 128), 0) == 0
    lying = [jnp.transpose(tile_of(128, [k[i * rows : (i + 1) * rows]])) for i in range(n_x)]
    quarter = max(1, second.shape[0] // 4)
    for q in range(0, second.shape[0], quarter):
        for j in range(q, q + quarter):
            for i in range(n_x):
                d, part = j * n_x + i, slice(i * rows, (i + 1) * rows)
                out[d, 0:rows] = whole(stash[j, part] * up[part, j : j + 1])
                out[d, rows : rows + 8] = whole(jnp.where(top_row, lying[i][j : j + 1], tail))
        piece = slice(q * n_x, (q + quarter) * n_x)
        sem = sems.at[n_x + q // quarter]
        copies.append(pltpu.make_async_copy(out.at[piece], out_hbm.at[piece], sem))
        copies[-1].start()
    for copy in copies:
        copy.wait()


def across_kernel(served, got, own, from_1, from_2, from_3, out, sums, parted):
    n_x, n_z = served.shape[0], out.shape[0]
    wide = out.shape[1] - 8
    few = wide // 16
    size, rows = own.shape[0], n_z * few
    parts = size // 128

    sides = (from_1, from_2, from_3)
    exps = [real(ref[size : size + 8])[0:parts] for ref in sides]
    down = jnp.transpose(tile_of(128, exps))
    down = scale_of(down) * (1.0 / LEVELS)
    for t in range(parts):
        part = slice(t * 128, (t + 1) * 128)
        total = own[part]
        for i, ref in enumerate(sides):
            lane = i * parts + t
            total = total + real(ref[part]) * down[:, lane : lane + 1]
        sums[part] = total

    tiles = [real(got[d, rows : rows + 8]) for d in range(got.shape[0])]
    down = scale_of(upright([t[0:1] for t in tiles], rows)) * (1.0 / LEVELS)
    for q in range(0, got.shape[0], 8):
        values = [real(got[d, 0:rows]) * down[:, d : d + 1] for d in range(q, q + 8)]
        for d, value in zip(range(q, q + 8), values):
            field = served[d % n_x, SPARE + d // n_x]
            at = pl.ds(pl.multiple_of(field * rows, 8), rows)
            sums[at] += value
    for f in range(16):
        for z in range(n_z):
            start = f * rows + z * few
            parted[z, f * few : (f + 1) * few] = sums[start : start + few]
    lanes = iota((wide, 128), 1)
    tops = jnp.zeros((wide, 128), f32)
    for z in range(n_z):
        tops = jnp.where(lanes == z, peaks(parted[z]), tops)
    k = exponent(tops)
    up = LEVELS * scale_of(-k)
    if wide < 128:
        k = tile_of(128, [k])
    lying = [jnp.transpose(k[n * 128 : (n + 1) * 128]) for n in range(k.shape[0] // 128)]
    common = digits(undigits(tiles, 1))
    for z in range(n_z):
        out[z, 0:wide] = whole(parted[z] * up[:, z : z + 1])
        mine = [part[z : z + 1] for part in lying]
        out[z, wide : wide + 8] = whole(tile_of(8, mine + common))


def last_kernel(
    scale, rate, tab, ft, second, mats_hbm, got, first_sums, targets,
    logits, grads, mats, errs, sums, mats_in, sem,
):
    load = pltpu.make_async_copy(mats_hbm, mats_in, sem)
    load.start()
    samples = second.shape[1]
    few = grads.shape[0]
    wide = 16 * few
    tiles = [real(got[i, wide : wide + 8]) for i in range(got.shape[0])]
    high = -(-wide // 128)
    exps = [upright([t[n : n + 1] for t in tiles], min(wide, 128)) for n in range(high)]
    down = scale_of(jnp.concatenate(exps, axis=0)) * (1.0 / LEVELS)
    value = scale * undigits(tiles, high)
    logits[...] = value
    errors = jax.nn.sigmoid(value) - targets[...]
    errs[...] = spread(errors, samples)
    total = real(got[0, 0:wide]) * down[:, 0:1]
    for i in range(1, got.shape[0]):
        total = total + real(got[i, 0:wide]) * down[:, i : i + 1]
    sums[...] = total * (1.0 / math.sqrt(128.0))
    for b in range(few):
        mine = errs[pl.ds(tab[MY_OWN, 0] * few + b, 1)]
        grads[b] = sums[pl.ds(b, 16, stride=few)] * mine
    earlier = jax.nn.sigmoid(scale * total_of(first_sums)) - targets[...]
    errs[...] = spread(errors + earlier, samples)

    group = math.gcd(LAST_GROUP, second.shape[0])
    load.wait()

    def step(q, carry):
        js = [q * group + i for i in range(group)]
        e = errs[...]
        both = [dot(ft[tab[FIRST, j]], beside(second[j].astype(f32) * e), ATB) for j in js]
        for j, g in zip(js, both):
            slot, live = tab[SLOT, j], tab[LIVE, j].astype(f32)
            mats[slot] = mats_in[slot] - (rate * live) * (g[:, :128] + g[:, 128:])
        return carry

    lax.fori_loop(0, second.shape[0] // group, step, 0)


def call(kernel, outs, n_in, scratch=(), smem=True, far_in=(), far_out=False, room=16):
    specs = [pl.BlockSpec(memory_space=pltpu.VMEM)] * n_in
    if smem:
        specs[0] = pl.BlockSpec(memory_space=pltpu.SMEM)
    for i in far_in:
        specs[i] = pl.BlockSpec(memory_space=pltpu.HBM)
    space = pltpu.HBM if far_out else pltpu.VMEM
    return pl.pallas_call(
        kernel,
        out_shape=[pltpu.HBM(o.shape, o.dtype) for o in outs] if far_out else outs,
        in_specs=specs,
        out_specs=[pl.BlockSpec(memory_space=space)] * len(outs),
        scratch_shapes=list(scratch),
        compiler_params=pltpu.CompilerParams(vmem_limit_bytes=room << 20),
    )


def shape(dims, dtype=f32):
    return jax.ShapeDtypeStruct(dims, dtype)


def swap(x, axes):
    return lax.all_to_all(x, axes, split_axis=0, concat_axis=0, tiled=True)


def on_device(fields, labels, pair_first, pair_second, pair_count, pair_mats):
    groups, owners = lax.axis_size(GRP), lax.axis_size(OWN)
    n_x, n_z = lax.axis_size("x"), lax.axis_size("z")
    me = lax.axis_index(GRP)
    samples, per_block, feature = fields.shape
    slots = pair_first.shape[2]
    scale = logit_gain / math.sqrt(groups * owners * slots)
    rate = step_size * scale / (samples * feature)
    few = samples // owners

    table = pair_second[:, 0, :]
    blocks = table // per_block
    served = jnp.sum(jnp.where(blocks == me, table - me * per_block, 0), axis=1)
    mine = lax.dynamic_index_in_dim(blocks, me, 0, keepdims=False)
    picked = mine[:, None] == jnp.arange(slots, dtype=jnp.int32)[None, :]
    slot_ids = jnp.arange(slots, dtype=jnp.int32)[:, None]
    slot_of = jnp.sum(jnp.where(picked, slot_ids, 0), axis=0)
    first_of = jnp.sum(jnp.where(picked, (pair_first[0, 0] - me * per_block)[:, None], 0), axis=0)
    live = (slot_of < pair_count[0, 0]).astype(jnp.int32)
    places = [lax.axis_index(OWN), lax.axis_index("x")]
    places = [jnp.full((slots,), place, jnp.int32) for place in places]
    tab = jnp.stack([slot_of, first_of, live, served] + places)

    ft = jnp.transpose(fields, (1, 0, 2))
    mats = pair_mats[0, 0]
    row = pltpu.with_memory_space_constraint(labels.reshape(1, samples), pltpu.HBM)

    sent = call(gather_kernel, [shape((slots, samples, feature), bf16)], 2)(tab, ft)[0]
    second = swap(sent, GRP)
    acc = pltpu.VMEM((samples, 128), f32)
    out = [shape((groups * n_x, 2, 128)), shape((2, 128))]
    room = [acc, pltpu.VMEM((1, samples), jnp.int32), pltpu.SemaphoreType.DMA(())]
    call_partial = call(partial_kernel, out, 5, room, far_in=(4,))
    part, targets = call_partial(tab, ft, second, mats, row)
    out = [shape((n_z, 2, 128)), shape((n_x, 128), jnp.int32)]
    part, near = call(sum_kernel, out, 1, smem=False)(swap(part, GRP + ("x",)))
    sums = swap(part, "z")

    rows, wide = samples // n_x, per_block * few
    size = per_block * rows
    side = shape((size + 8, feature), jnp.int16)
    out, own, *sides = call(
        functools.partial(terms_kernel, scale, rate),
        [
            shape((groups * n_x, rows + 8, feature), jnp.int16),
            shape((size, feature)),
            side,
            side,
            side,
        ],
        6,
        [
            acc,
            acc,
            pltpu.VMEM((slots, samples, feature), f32),
            acc,
            pltpu.VMEM((n_x, size, feature), f32),
            pltpu.VMEM((groups * n_x, rows + 8, feature), jnp.int16),
            pltpu.VMEM((n_x - 1, size + 8, feature), jnp.int16),
            pltpu.SemaphoreType.DMA((n_x + 4,)),
        ],
        far_out=True,
        room=24,
    )(tab, ft, second, mats, sums, targets)
    got = swap(out, GRP + ("x",))
    sides = [
        lax.ppermute(side, "x", [(i, (i + r) % n_x) for i in range(n_x)])
        for r, side in enumerate(sides, 1)
    ]
    out = [shape((n_z, wide + 8, feature), jnp.int16)]
    room = [pltpu.VMEM((size, feature), f32), pltpu.VMEM((n_z, wide, feature), f32)]
    got = call(across_kernel, out, 6, room, room=16)(near, got, own, *sides)[0]
    got = swap(got, "z")
    logits, grads, mats = call(
        functools.partial(last_kernel, scale, rate),
        [shape((2, 128)), shape((few, per_block, feature)), shape(mats.shape)],
        7,
        [
            acc,
            pltpu.VMEM((per_block * few, 128), f32),
            pltpu.VMEM(mats.shape, f32),
            pltpu.SemaphoreType.DMA(()),
        ],
        far_in=(3,),
    )(tab, ft, second, pltpu.with_memory_space_constraint(pair_mats[0, 0], pltpu.HBM), got, sums, targets)
    return logits.reshape(256)[:samples], grads, mats[None, None]


def solution(mesh):
    n_grp, n_own = mesh.devices.shape
    sizes = (n_grp // 2, 2, 4, n_own // 4)
    split_mesh = Mesh(mesh.devices.reshape(sizes), ("y", "core", "x", "z"))
    in_specs = (
        P(None, GRP, None),
        P(),
        P(GRP, OWN, None),
        P(None, OWN, None),
        P(GRP, OWN),
        P(GRP, OWN, None, None, None),
    )
    out_specs = (P(), P(OWN, GRP, None), P(GRP, OWN, None, None, None))
    return jax.shard_map(
        on_device, mesh=split_mesh, in_specs=in_specs, out_specs=out_specs, check_vma=False
    )
```

```python
import functools
import math

import jax
import jax.numpy as jnp
from jax import lax
from jax.experimental import pallas as pl
from jax.experimental.pallas import tpu as pltpu
from jax.sharding import Mesh
from jax.sharding import PartitionSpec as P

GRP = ("y", "core")
OWN = ("x", "z")
logit_gain = 1.5
step_size = 1000.0
f32 = jnp.float32
bf16 = jnp.bfloat16

SLOT, FIRST, LIVE, SERVED, MY_OWN, MY_X = range(6)

PARTIAL_GROUP, TERMS_GROUP, LAST_GROUP = 16, 16, 16
SPARE = 64


def split(x):
    hi = x.astype(bf16)
    return hi, (x - hi.astype(f32)).astype(bf16)


def dot(a, b, dims):
    return lax.dot_general(a, b, (dims, ((), ())), preferred_element_type=f32)


def beside(x):
    return jnp.concatenate(split(x), axis=1)


def twice(x):
    return jnp.concatenate([x, x], axis=1)


AB, ABT, ATB = ((1,), (0,)), ((1,), (1,)), ((0,), (0,))


def row_sums(acc):
    ones = jnp.ones((8, 128), f32)
    exact = functools.partial(
        lax.dot_general,
        dimension_numbers=(ABT, ((), ())),
        precision=lax.Precision.HIGHEST,
        preferred_element_type=f32,
    )
    low = exact(ones, acc[:128])
    rest = acc[128:]
    high = exact(ones, jnp.concatenate([rest, jnp.zeros((256 - acc.shape[0], 128), f32)], axis=0))
    return jnp.concatenate([low[0:1], high[0:1]], axis=0)


def spread(chunk, samples):
    low = jnp.transpose(jnp.broadcast_to(chunk[0:1], (128, 128)))
    high = jnp.transpose(jnp.broadcast_to(chunk[1:2], (128, 128)))
    return jnp.concatenate([low, high[: samples - 128]], axis=0)


def gather_kernel(tab, ft, out):
    @pl.loop(0, out.shape[0])
    def _(j):
        out[j] = ft[tab[SERVED, j]]


def partial_kernel(tab, ft, second, mats, labels_hbm, out, targets, acc, labels, sem):
    load = pltpu.make_async_copy(labels_hbm, labels, sem)
    load.start()
    acc[...] = jnp.zeros_like(acc)

    group = math.gcd(PARTIAL_GROUP, second.shape[0])

    def step(q, carry):
        js = [q * group + i for i in range(group)]
        pairs = [split(mats[tab[SLOT, j]] * tab[LIVE, j].astype(f32)) for j in js]
        mixed = [
            dot(twice(ft[tab[FIRST, j]]), jnp.concatenate(pair, axis=0), AB)
            for j, pair in zip(js, pairs)
        ]
        total = acc[...]
        for j, m in zip(js, mixed):
            total = total + m * second[j].astype(f32)
        acc[...] = total
        return carry

    lax.fori_loop(0, second.shape[0] // group, step, 0)
    chunk = row_sums(acc[...] * (1.0 / 128.0))
    lanes = iota((2, 128), 1) + 128 * (1 - iota((2, 128), 0))
    for j in range(second.shape[0]):
        chunk = jnp.where(lanes == SPARE + j, tab[SERVED, j].astype(f32), chunk)
    for i in range(out.shape[0]):
        out[i] = chunk
    load.wait()
    targets[...] = folded(labels)


def sum_kernel(parts, out, served):
    total = total_of(parts)
    for i in range(out.shape[0]):
        out[i] = total
    n_x = served.shape[0]
    near = parts[pl.ds(lax.axis_index(GRP) * n_x, n_x)]
    lanes = iota((1, 128), 1)
    mine = (lanes >= SPARE) & (lanes < SPARE + 16)
    for i in range(n_x):
        served[i : i + 1] = jnp.where(mine, near[i, 1:2], 0.0).astype(jnp.int32)


def folded(labels):
    row = labels[...].astype(f32)
    rest = jnp.zeros((1, 256 - row.shape[1]), f32)
    return jnp.concatenate([row[:, :128], jnp.concatenate([row[:, 128:], rest], axis=1)], axis=0)


def total_of(parts):
    total = parts[0]
    for i in range(1, parts.shape[0]):
        total = total + parts[i]
    return total


LEVELS = 32000.0
OCTAVE = 64.0


def exponent(peak):
    return jnp.ceil(OCTAVE * jnp.log2(jnp.maximum(peak, 1e-30)))


def scale_of(k):
    return jnp.exp2(k * (1.0 / OCTAVE))


def whole(x):
    return jnp.round(x).astype(jnp.int32).astype(jnp.int16)


def real(x):
    return x.astype(jnp.int32).astype(f32)


def peaks(x):
    return jnp.max(jnp.abs(x), axis=1, keepdims=True)


def iota(dims, axis):
    return lax.broadcasted_iota(jnp.int32, dims, axis)


def tile_of(height, pieces):
    used = sum(p.shape[0] for p in pieces)
    return jnp.concatenate(pieces + [jnp.zeros((height - used, 128), f32)], axis=0)


def digits(pair):
    k = exponent(jnp.max(peaks(pair), axis=0, keepdims=True))
    wide = pair * (LEVELS * scale_of(-k))
    high = jnp.round(wide)
    return [high, (wide - high) * LEVELS, jnp.broadcast_to(k, (1, 128))]


def undigit(tile, at):
    s = scale_of(tile[at + 4 : at + 5]) * (1.0 / LEVELS)
    return s * (tile[at : at + 2] + tile[at + 2 : at + 4] * (1.0 / LEVELS))


def undigits(tiles, at):
    total = undigit(tiles[0], at)
    for t in tiles[1:]:
        total = total + undigit(t, at)
    return total


def upright(rows, height):
    tall = jnp.concatenate(rows + [jnp.zeros((128 - len(rows), 128), f32)], axis=0)
    return jnp.transpose(tall)[:height]


def terms_kernel(
    scale, rate, tab, ft, second, mats, sums, targets,
    out_hbm, own_hbm, to_1, to_2, to_3,
    acc, errs, stash, tops, dense, out, to_all, sems,
):
    samples = second.shape[1]
    n_x, size = dense.shape[0], dense.shape[1]
    rows, parts = samples // n_x, size // 128
    errors = jax.nn.sigmoid(scale * total_of(sums)) - targets[...]
    errs[...] = spread(errors, samples)
    acc[...] = jnp.zeros_like(acc)
    dense[...] = jnp.zeros_like(dense)
    tops[...] = jnp.zeros_like(tops)
    lanes = iota((samples, 128), 1)

    group = math.gcd(TERMS_GROUP, second.shape[0])

    def step(q, carry):
        js = [q * group + i for i in range(group)]
        lives = [tab[LIVE, j].astype(f32) for j in js]
        slots = [tab[SLOT, j] for j in js]
        firsts = [tab[FIRST, j] for j in js]
        vas, vbs = [ft[first] for first in firsts], [second[j] for j in js]
        e = errs[...]
        both = [dot(va, beside(vb.astype(f32) * e), ATB) for va, vb in zip(vas, vbs)]
        updated = [
            (mats[slot] - (rate * live) * (g[:, :128] + g[:, 128:])) * live
            for slot, live, g in zip(slots, lives, both)
        ]
        pairs = [split(m) for m in updated]
        mixed = [
            dot(twice(va), jnp.concatenate(pair, axis=0), AB) for va, pair in zip(vas, pairs)
        ]
        toward = [
            dot(twice(vb), jnp.concatenate(pair, axis=1), ABT) for vb, pair in zip(vbs, pairs)
        ]
        total, top = acc[...], tops[...]
        for j, m, vb in zip(js, mixed, vbs):
            stash[j] = m
            total = total + m * vb.astype(f32)
            top = jnp.where(lanes == j, peaks(m), top)
        acc[...] = total
        tops[...] = top
        for first, t in zip(firsts, toward):
            at = pl.ds(pl.multiple_of(first * rows, 8), rows)
            for i in range(n_x):
                dense[i, at] += t[i * rows : (i + 1) * rows]
        return carry

    lax.fori_loop(0, second.shape[0] // group, step, 0)

    x = tab[MY_X, 0]
    copies = [pltpu.make_async_copy(dense.at[x], own_hbm, sems.at[0])]
    copies[0].start()
    lanes = iota((128, 128), 1)
    far = [lax.rem(x + r, n_x) for r in range(1, n_x)]
    high = jnp.zeros((128, 128), f32)
    for i, to in enumerate(far):
        for t in range(parts):
            top = peaks(dense[to, t * 128 : (t + 1) * 128])
            high = jnp.where(lanes == i * parts + t, top, high)
    k = exponent(high)
    up = LEVELS * scale_of(-k)
    lying = jnp.transpose(k)
    for i, (to, ref) in enumerate(zip(far, (to_1, to_2, to_3))):
        for t in range(parts):
            lane = i * parts + t
            part = dense[to, t * 128 : (t + 1) * 128]
            to_all[i, t * 128 : (t + 1) * 128] = whole(part * up[:, lane : lane + 1])
        mine = lying[i * parts : (i + 1) * parts]
        to_all[i, size : size + 8] = whole(tile_of(8, [mine]))
        copies.append(pltpu.make_async_copy(to_all.at[i], ref, sems.at[1 + i]))
        copies[-1].start()

    k = exponent(tops[...])
    up = LEVELS * scale_of(-k)
    zero = jnp.zeros((1, 128), f32)
    tail = tile_of(8, [zero] + digits(row_sums(acc[...] * (1.0 / 128.0))))
    top_row = iota((8, 128), 0) == 0
    lying = [jnp.transpose(tile_of(128, [k[i * rows : (i + 1) * rows]])) for i in range(n_x)]
    quarter = max(1, second.shape[0] // 4)
    for q in range(0, second.shape[0], quarter):
        for j in range(q, q + quarter):
            for i in range(n_x):
                d, part = j * n_x + i, slice(i * rows, (i + 1) * rows)
                out[d, 0:rows] = whole(stash[j, part] * up[part, j : j + 1])
                out[d, rows : rows + 8] = whole(jnp.where(top_row, lying[i][j : j + 1], tail))
        piece = slice(q * n_x, (q + quarter) * n_x)
        sem = sems.at[n_x + q // quarter]
        copies.append(pltpu.make_async_copy(out.at[piece], out_hbm.at[piece], sem))
        copies[-1].start()
    for copy in copies:
        copy.wait()


def across_kernel(served, got, own, from_1, from_2, from_3, out, sums, parted):
    n_x, n_z = served.shape[0], out.shape[0]
    wide = out.shape[1] - 8
    few = wide // 16
    size, rows = own.shape[0], n_z * few
    parts = size // 128

    sides = (from_1, from_2, from_3)
    exps = [real(ref[size : size + 8])[0:parts] for ref in sides]
    down = jnp.transpose(tile_of(128, exps))
    down = scale_of(down) * (1.0 / LEVELS)
    for t in range(parts):
        part = slice(t * 128, (t + 1) * 128)
        total = own[part]
        for i, ref in enumerate(sides):
            lane = i * parts + t
            total = total + real(ref[part]) * down[:, lane : lane + 1]
        sums[part] = total

    tiles = [real(got[d, rows : rows + 8]) for d in range(got.shape[0])]
    down = scale_of(upright([t[0:1] for t in tiles], rows)) * (1.0 / LEVELS)
    for q in range(0, got.shape[0], 8):
        values = [real(got[d, 0:rows]) * down[:, d : d + 1] for d in range(q, q + 8)]
        for d, value in zip(range(q, q + 8), values):
            field = served[d % n_x, SPARE + d // n_x]
            at = pl.ds(pl.multiple_of(field * rows, 8), rows)
            sums[at] += value
    for f in range(16):
        for z in range(n_z):
            start = f * rows + z * few
            parted[z, f * few : (f + 1) * few] = sums[start : start + few]
    lanes = iota((wide, 128), 1)
    tops = jnp.zeros((wide, 128), f32)
    for z in range(n_z):
        tops = jnp.where(lanes == z, peaks(parted[z]), tops)
    k = exponent(tops)
    up = LEVELS * scale_of(-k)
    if wide < 128:
        k = tile_of(128, [k])
    lying = [jnp.transpose(k[n * 128 : (n + 1) * 128]) for n in range(k.shape[0] // 128)]
    common = digits(undigits(tiles, 1))
    for z in range(n_z):
        out[z, 0:wide] = whole(parted[z] * up[:, z : z + 1])
        mine = [part[z : z + 1] for part in lying]
        out[z, wide : wide + 8] = whole(tile_of(8, mine + common))


def last_kernel(
    scale, rate, tab, ft, second, mats_hbm, got, first_sums, targets,
    logits, grads, mats, errs, sums, mats_in, sems,
):
    count = mats_in.shape[0] // sems.shape[0]
    loads = [
        pltpu.make_async_copy(mats_hbm.at[part], mats_in.at[part], sems.at[i])
        for i, part in enumerate(pl.ds(i * count, count) for i in range(sems.shape[0]))
    ]
    for load in loads:
        load.start()
    samples = second.shape[1]
    few = grads.shape[0]
    wide = 16 * few
    tiles = [real(got[i, wide : wide + 8]) for i in range(got.shape[0])]
    high = -(-wide // 128)
    exps = [upright([t[n : n + 1] for t in tiles], min(wide, 128)) for n in range(high)]
    down = scale_of(jnp.concatenate(exps, axis=0)) * (1.0 / LEVELS)
    value = scale * undigits(tiles, high)
    logits[...] = value
    errors = jax.nn.sigmoid(value) - targets[...]
    errs[...] = spread(errors, samples)
    total = real(got[0, 0:wide]) * down[:, 0:1]
    for i in range(1, got.shape[0]):
        total = total + real(got[i, 0:wide]) * down[:, i : i + 1]
    sums[...] = total * (1.0 / math.sqrt(128.0))
    for b in range(few):
        mine = errs[pl.ds(tab[MY_OWN, 0] * few + b, 1)]
        grads[b] = sums[pl.ds(b, 16, stride=few)] * mine
    earlier = jax.nn.sigmoid(scale * total_of(first_sums)) - targets[...]
    errs[...] = spread(errors + earlier, samples)

    group = math.gcd(LAST_GROUP, second.shape[0])
    for load in loads:
        load.wait()

    def step(q, carry):
        js = [q * group + i for i in range(group)]
        e = errs[...]
        both = [dot(ft[tab[FIRST, j]], beside(second[j].astype(f32) * e), ATB) for j in js]
        for j, g in zip(js, both):
            slot, live = tab[SLOT, j], tab[LIVE, j].astype(f32)
            mats[slot] = mats_in[slot] - (rate * live) * (g[:, :128] + g[:, 128:])
        return carry

    lax.fori_loop(0, second.shape[0] // group, step, 0)


def call(kernel, outs, n_in, scratch=(), smem=True, far_in=(), far_out=False, room=16):
    specs = [pl.BlockSpec(memory_space=pltpu.VMEM)] * n_in
    if smem:
        specs[0] = pl.BlockSpec(memory_space=pltpu.SMEM)
    for i in far_in:
        specs[i] = pl.BlockSpec(memory_space=pltpu.HBM)
    space = pltpu.HBM if far_out else pltpu.VMEM
    return pl.pallas_call(
        kernel,
        out_shape=[pltpu.HBM(o.shape, o.dtype) for o in outs] if far_out else outs,
        in_specs=specs,
        out_specs=[pl.BlockSpec(memory_space=space)] * len(outs),
        scratch_shapes=list(scratch),
        compiler_params=pltpu.CompilerParams(vmem_limit_bytes=room << 20),
    )


def shape(dims, dtype=f32):
    return jax.ShapeDtypeStruct(dims, dtype)


def swap(x, axes):
    return lax.all_to_all(x, axes, split_axis=0, concat_axis=0, tiled=True)


def on_device(fields, labels, pair_first, pair_second, pair_count, pair_mats):
    groups, owners = lax.axis_size(GRP), lax.axis_size(OWN)
    n_x, n_z = lax.axis_size("x"), lax.axis_size("z")
    me = lax.axis_index(GRP)
    samples, per_block, feature = fields.shape
    slots = pair_first.shape[2]
    scale = logit_gain / math.sqrt(groups * owners * slots)
    rate = step_size * scale / (samples * feature)
    few = samples // owners

    table = pair_second[:, 0, :]
    blocks = table // per_block
    served = jnp.sum(jnp.where(blocks == me, table - me * per_block, 0), axis=1)
    mine = lax.dynamic_index_in_dim(blocks, me, 0, keepdims=False)
    picked = mine[:, None] == jnp.arange(slots, dtype=jnp.int32)[None, :]
    slot_ids = jnp.arange(slots, dtype=jnp.int32)[:, None]
    slot_of = jnp.sum(jnp.where(picked, slot_ids, 0), axis=0)
    first_of = jnp.sum(jnp.where(picked, (pair_first[0, 0] - me * per_block)[:, None], 0), axis=0)
    live = (slot_of < pair_count[0, 0]).astype(jnp.int32)
    places = [lax.axis_index(OWN), lax.axis_index("x")]
    places = [jnp.full((slots,), place, jnp.int32) for place in places]
    tab = jnp.stack([slot_of, first_of, live, served] + places)

    ft = jnp.transpose(fields, (1, 0, 2))
    mats = pair_mats[0, 0]
    row = pltpu.with_memory_space_constraint(labels.reshape(1, samples), pltpu.HBM)

    sent = call(gather_kernel, [shape((slots, samples, feature), bf16)], 2)(tab, ft)[0]
    second = swap(sent, GRP)
    acc = pltpu.VMEM((samples, 128), f32)
    out = [shape((groups * n_x, 2, 128)), shape((2, 128))]
    room = [acc, pltpu.VMEM((1, samples), jnp.int32), pltpu.SemaphoreType.DMA(())]
    call_partial = call(partial_kernel, out, 5, room, far_in=(4,))
    part, targets = call_partial(tab, ft, second, mats, row)
    out = [shape((n_z, 2, 128)), shape((n_x, 128), jnp.int32)]
    part, near = call(sum_kernel, out, 1, smem=False)(swap(part, GRP + ("x",)))
    sums = swap(part, "z")

    rows, wide = samples // n_x, per_block * few
    size = per_block * rows
    side = shape((size + 8, feature), jnp.int16)
    out, own, *sides = call(
        functools.partial(terms_kernel, scale, rate),
        [
            shape((groups * n_x, rows + 8, feature), jnp.int16),
            shape((size, feature)),
            side,
            side,
            side,
        ],
        6,
        [
            acc,
            acc,
            pltpu.VMEM((slots, samples, feature), f32),
            acc,
            pltpu.VMEM((n_x, size, feature), f32),
            pltpu.VMEM((groups * n_x, rows + 8, feature), jnp.int16),
            pltpu.VMEM((n_x - 1, size + 8, feature), jnp.int16),
            pltpu.SemaphoreType.DMA((n_x + 4,)),
        ],
        far_out=True,
        room=24,
    )(tab, ft, second, mats, sums, targets)
    got = swap(out, GRP + ("x",))
    sides = [
        lax.ppermute(side, "x", [(i, (i + r) % n_x) for i in range(n_x)])
        for r, side in enumerate(sides, 1)
    ]
    out = [shape((n_z, wide + 8, feature), jnp.int16)]
    room = [pltpu.VMEM((size, feature), f32), pltpu.VMEM((n_z, wide, feature), f32)]
    got = call(across_kernel, out, 6, room, room=16)(near, got, own, *sides)[0]
    got = swap(got, "z")
    logits, grads, mats = call(
        functools.partial(last_kernel, scale, rate),
        [shape((2, 128)), shape((few, per_block, feature)), shape(mats.shape)],
        7,
        [
            acc,
            pltpu.VMEM((per_block * few, 128), f32),
            pltpu.VMEM(mats.shape, f32),
            pltpu.SemaphoreType.DMA((math.gcd(4, slots),)),
        ],
        far_in=(3,),
    )(tab, ft, second, pltpu.with_memory_space_constraint(pair_mats[0, 0], pltpu.HBM), got, sums, targets)
    return logits.reshape(256)[:samples], grads, mats[None, None]


def solution(mesh):
    n_grp, n_own = mesh.devices.shape
    sizes = (n_grp // 2, 2, 4, n_own // 4)
    split_mesh = Mesh(mesh.devices.reshape(sizes), ("y", "core", "x", "z"))
    in_specs = (
        P(None, GRP, None),
        P(),
        P(GRP, OWN, None),
        P(None, OWN, None),
        P(GRP, OWN),
        P(GRP, OWN, None, None, None),
    )
    out_specs = (P(), P(OWN, GRP, None), P(GRP, OWN, None, None, None))
    return jax.shard_map(
        on_device, mesh=split_mesh, in_specs=in_specs, out_specs=out_specs, check_vma=False
    )
```
